1024 devices in a mesh: ctx: 128 (over y, x, core), tp: 8 (over z).
Axes of the slice: x: 8, y: 8, z: 8, core: 2. Of those that a mesh axis runs over, the one named last changes fastest.
Arguments:
- hidden_in: bfloat16 [16384, 4096], P('ctx'), may hold values from -6 to 6
- in_proj: bfloat16 [4096, 3, 2048], P(None, None, 'tp'), may hold values from -1 to 1
- short_taps: bfloat16 [3, 3, 2048], P(None, None, 'tp'), may hold values from -2.5 to 2.5
- long_filters: float32 [16384, 128], P('ctx', 'tp'), may hold values from -2 to 2
- skip_gain: float32 [2048], P('tp'), may hold values from 0.5 to 1.5
- out_proj: bfloat16 [2048, 4096], P(None, 'tp'), may hold values from -1 to 1
Outputs:
- block_out: bfloat16 [16384, 4096], P('ctx', 'tp')
The draws below stay inside these ranges and needn't reach their ends.
All inputs are finite; a program needn't handle non-finite values.
Results may differ from the reference program's by a relative error of at most 0.015.
Values may be sent and summed in bfloat16 or wider, within the bound.
A program may use at most 64 MiB of HBM per device.

```python
import math
import jax
import jax.numpy as jnp
from jax import lax

D = 4096
CH = 2048
FG = 16
KS = 3
SEQ = 16384
NF = 128


def draw_long_filters(key, part):
    base = jax.random.fold_in(key, 7)
    noise_key, reach_key = jax.random.split(base)
    noise = jax.random.truncated_normal(noise_key, -4.0, 4.0, (SEQ, NF), jnp.float32)
    lowest = SEQ / 4.0
    highest = 2.0 * SEQ
    reach = jnp.exp(jax.random.uniform(reach_key, (1, NF), jnp.float32, math.log(lowest), math.log(highest)))
    lag = jnp.arange(SEQ, dtype=jnp.float32)[:, None]
    amplitude = jnp.sqrt(jnp.expm1(-2.0 / reach) / jnp.expm1(-2.0 * SEQ / reach))
    return noise * jnp.exp(-lag / reach) * amplitude


def draw_in_proj(key, part):
    base = jax.random.fold_in(key, 11)
    scale = 1.0 / math.sqrt(D)
    values = jax.random.truncated_normal(base, -4.0, 4.0, (D, 3, CH), jnp.float32)
    return (values * scale).astype(jnp.bfloat16)


def draw_short_taps(key, part):
    base = jax.random.fold_in(key, 13)
    scale = 1.0 / math.sqrt(KS)
    values = jax.random.truncated_normal(base, -4.0, 4.0, (KS, 3, CH), jnp.float32)
    return (values * scale).astype(jnp.bfloat16)


def draw_out_proj(key, part):
    base = jax.random.fold_in(key, 17)
    scale = 1.0 / math.sqrt(CH)
    values = jax.random.truncated_normal(base, -4.0, 4.0, (CH, D), jnp.float32)
    return (values * scale).astype(jnp.bfloat16)


def levels(own_key, extent, shards, least, high):
    def one(dim, parts):
        draws = jax.random.uniform(jax.random.fold_in(jax.random.fold_in(own_key, 6), dim), (parts,), jnp.float32, least / len(shards), high / len(shards))
        return jnp.repeat(jnp.exp(draws), extent[dim] // parts).reshape((-1,) + (1,) * (len(extent) - dim - 1))

    gain = one(*shards[0])
    for cut in shards[1:]:
        gain = gain * one(*cut)
    return gain


def scatter_about(stream_key, dims, spread, most, pieces=(), kind=jnp.bfloat16):
    values = spread * jax.random.normal(stream_key, dims, jnp.float32)
    if pieces:
        values = values * levels(stream_key, dims, pieces, -0.22, 0.18)
    return jnp.clip(values, -most, most).astype(kind)


def setup_inputs(seed: int = 0) -> dict:
    splits = jax.random.split(jax.random.key(seed), 7)
    hidden_in = scatter_about(splits[0], (SEQ, D), 1.0, 6.0, ((0, 128),))
    in_proj = draw_in_proj(jax.random.fold_in(splits[6], 71), 0)
    short_taps = draw_short_taps(jax.random.fold_in(splits[6], 71), 0)
    long_filters = draw_long_filters(jax.random.fold_in(splits[6], 71), 0)
    skip_gain = jnp.clip(0.5 + 1.0 * jax.random.uniform(splits[4], (CH,), jnp.float32) ** levels(splits[4], (CH,), ((0, 8),), -0.2, 0.2), 0.5, 1.5)
    out_proj = draw_out_proj(jax.random.fold_in(splits[6], 71), 0)
    return {"hidden_in": hidden_in, "in_proj": in_proj, "short_taps": short_taps, "long_filters": long_filters, "skip_gain": skip_gain, "out_proj": out_proj}


def reference(hidden_in, in_proj, short_taps, long_filters, skip_gain, out_proj):
    proj = jnp.dot(hidden_in, in_proj.reshape(D, 3 * CH), preferred_element_type=jnp.float32)
    proj = lax.optimization_barrier(proj.astype(jnp.bfloat16)).reshape(SEQ, 3, CH)
    padded = jnp.concatenate([jnp.zeros((KS - 1, 3, CH), jnp.bfloat16), proj], 0).astype(jnp.float32)
    taps = short_taps.astype(jnp.float32)
    feat = jnp.zeros((SEQ, 3, CH), jnp.float32)
    for shift_back in range(KS):
        start = KS - 1 - shift_back
        feat = feat + taps[shift_back][None] * padded[start:start + SEQ]
    query = feat[:, 0, :]
    gated = feat[:, 1, :] * feat[:, 2, :]
    length = 2 * SEQ
    spec_signal = jnp.fft.rfft(gated, n=length, axis=0)
    spec_filter = jnp.repeat(jnp.fft.rfft(long_filters, n=length, axis=0), FG, axis=1)
    conv = jnp.fft.irfft(spec_signal * spec_filter, n=length, axis=0)[:SEQ]
    hidden = (query * (conv + skip_gain[None, :] * gated)).astype(jnp.bfloat16)
    return jnp.dot(hidden, out_proj, preferred_element_type=jnp.float32).astype(jnp.bfloat16)
```

```python
import functools

import jax
import jax.numpy as jnp
from jax import lax
from jax.experimental import pallas as pl
from jax.experimental.pallas import tpu as pltpu
from jax.sharding import PartitionSpec as P

MESH = pl.DeviceIdType.MESH
NX = 16
NY = 8
NZ = 8
ROWS = 128
CHAN = 256
MODEL = 4096
FEATS = 512
KCH = 1024
NK = MODEL // KCH
TOEP = 16512


def kernel(
    x_hbm, w_hbm, taps_hbm, filt_hbm, skip_hbm, o_hbm, out_ref,
    xb, wb, ob, taps_v, filt_v, skip_v,
    pacc, halo_s, halo_r, ext, gated_v, query_v,
    fs, fr, hs, hr, toep, perm1, perm2, sel, lhs,
    xs, xr, ys, yr, acc, ys2, yr2, xs2, xr2, hid, oacc,
    in_sem, w_sem, halo_sem, f_sem, h_sem, x_sem, y_sem, y2_sem, x2_sem, zr_sem, zl_sem,
):
    f32, bf16 = jnp.float32, jnp.bfloat16
    ctx = lax.axis_index("ctx")
    z = lax.axis_index("tp")
    y, xc = ctx // NX, ctx % NX
    nxt, prv = (ctx + 1) % (NX * NY), (ctx + NX * NY - 1) % (NX * NY)
    zp, zm = (z + 1) % NZ, (z + NZ - 1) % NZ

    def rowpeer(o):
        return (xc + o) % NX

    def colpeer(o):
        return (y + o) % NY

    copies = [
        pltpu.make_async_copy(x_hbm, xb, in_sem.at[0]),
        pltpu.make_async_copy(taps_hbm, taps_v, in_sem.at[1]),
        pltpu.make_async_copy(filt_hbm, filt_v, in_sem.at[2]),
        pltpu.make_async_copy(skip_hbm, skip_v, in_sem.at[3]),
        pltpu.make_async_copy(o_hbm, ob, in_sem.at[4]),
    ]

    def wcopy(j, c):
        at = pl.ds(c * KCH, KCH)
        return pltpu.make_async_copy(w_hbm.at[j, at], wb.at[j, at], w_sem.at[j, c])

    copies[2].start()
    copies[0].start()
    for j in (1, 2, 0):
        for c in range(NK):
            wcopy(j, c).start()
    copies[1].start()
    copies[3].start()
    copies[4].start()

    barrier = pltpu.get_barrier_semaphore()
    for o in range(1, NX):
        pl.semaphore_signal(barrier, inc=1, device_id=(y * NX + rowpeer(o), z), device_id_type=MESH)
    for o in range(1, NY):
        pl.semaphore_signal(barrier, inc=1, device_id=(colpeer(o) * NX + xc, z), device_id_type=MESH)
    for peer in ((ctx, zp), (ctx, zm), (nxt, z), (prv, z)):
        pl.semaphore_signal(barrier, inc=1, device_id=peer, device_id_type=MESH)

    copies[2].wait()
    for f in range(NX):
        fs[f] = filt_v[f : f + 1, :]

    pl.semaphore_wait(barrier, NX - 1 + NY - 1 + 4)

    def send(src, dst, sems, k_send, k_recv, c, t):
        return pltpu.make_async_remote_copy(
            src_ref=src, dst_ref=dst, send_sem=sems.at[0, k_send], recv_sem=sems.at[1, k_recv],
            device_id=(c, t), device_id_type=MESH)

    sent = []

    def go(copy):
        copy.start()
        sent.append(copy)

    order_x = (8, 7, 9, 6, 10, 5, 11, 4, 12, 3, 13, 2, 14, 1, 15)
    order_y = (4, 3, 5, 2, 6, 1, 7)

    def row_exchange(src, dst, sems):
        for o in order_x:
            p = rowpeer(o)
            go(send(src.at[p], dst.at[xc], sems, o, o, y * NX + p, z))

    def row_arrive(dst, sems):
        for o in order_x:
            p = (xc + NX - o) % NX
            send(dst.at[p], dst.at[p], sems, o, o, ctx, z).wait_recv()

    def col_exchange(src_of, dst, sems):
        for o in order_y:
            p = colpeer(o)
            go(send(src_of(p), dst.at[y], sems, o, o, p * NX + xc, z))

    def col_arrive(dst, sems):
        for o in order_y:
            p = (y + NY - o) % NY
            send(dst.at[p], dst.at[p], sems, o, o, ctx, z).wait_recv()

    row_exchange(fs, fr, f_sem)
    fr[xc] = fs[xc]

    copies[0].wait()
    pacc[...] = jnp.zeros_like(pacc)

    def project(j):
        @pl.loop(0, NK)
        def _(c):
            wcopy(j, c).wait()
            at = pl.ds(pl.multiple_of(c * KCH, KCH), KCH)
            pacc[j] += jnp.dot(xb[:, at], wb[j, at, :], preferred_element_type=f32)

        rounded = pacc[j].astype(bf16)
        ext[j, 8:, :] = rounded.astype(f32)
        halo_s[j] = rounded[ROWS - 8 :, :]

    def halo(j):
        return send(halo_s.at[j], halo_r.at[j], halo_sem, j, j, nxt, z)

    def short_conv(j):
        send(halo_r.at[j], halo_r.at[j], halo_sem, j, j, ctx, z).wait_recv()
        before = halo_r[j].astype(f32)
        ext[j, :8, :] = jnp.where(ctx == 0, jnp.zeros_like(before), before)
        taps = [taps_v[i].astype(f32)[j : j + 1, :] for i in range(3)]
        return (
            taps[0] * ext[j, 8:, :]
            + taps[1] * ext[j, 7 : 7 + ROWS, :]
            + taps[2] * ext[j, 6 : 6 + ROWS, :]
        )

    project(1)
    go(halo(1))
    project(2)
    go(halo(2))
    copies[1].wait()
    keyed = short_conv(1)
    gated = keyed * short_conv(2)
    gated_v[...] = gated
    xs[...] = gated.T.astype(bf16).reshape(NX, 16, ROWS)
    row_exchange(xs, xr, x_sem)
    xr[xc] = xs[xc]

    row_arrive(fr, f_sem)
    hs[...] = fr[...].reshape(NX, ROWS)
    col_exchange(lambda p: hs, hr, h_sem)
    hr[y] = hs[...]

    row = lax.broadcasted_iota(jnp.int32, (256, 256), 0)
    col = lax.broadcasted_iota(jnp.int32, (256, 256), 1)
    perm1[...] = jnp.where(col == (row // 2 % 16) * 16 + row // 32 * 2 + row % 2, 1.0, 0.0).astype(bf16)
    row = lax.broadcasted_iota(jnp.int32, (128, 128), 0)
    col = lax.broadcasted_iota(jnp.int32, (128, 128), 1)
    perm2[...] = jnp.where(col == (row % 16 // 2) * 16 + row // 16 * 2 + row % 2, 1.0, 0.0).astype(bf16)
    row = lax.broadcasted_iota(jnp.int32, (128, 256), 0)
    col = lax.broadcasted_iota(jnp.int32, (128, 256), 1)
    base = row // 2 * 4 + row % 2 - col

    @pl.loop(0, 16)
    def _(b):
        shift = (7 - b // 2) * 4 - b % 2 * 2
        sel[pl.ds(pl.multiple_of(b * 128, 128), 128), :] = jnp.where(base == shift, 1.0, 0.0).astype(bf16)

    project(0)
    go(halo(0))
    query_v[...] = short_conv(0)

    row_arrive(xr, x_sem)
    ys[...] = jnp.dot(
        perm1[...], xr[...].reshape(256, ROWS), preferred_element_type=f32
    ).astype(bf16).reshape(NY, 32, ROWS)
    col_exchange(lambda p: ys.at[p], yr, y_sem)
    yr[y] = ys[y]

    col_arrive(hr, h_sem)
    lane = lax.broadcasted_iota(jnp.int32, (128, 128), 1)
    sub = lax.broadcasted_iota(jnp.int32, (128, 128), 0)
    keep = lane >= sub
    toep[128 * 128 :, :] = jnp.zeros((128, 128), bf16)

    def toeplitz(q, before):
        line = hr[q // 16, pl.ds(q % 16, 1), :]
        now = pltpu.roll(jnp.broadcast_to(line, (128, 128)), 0, 1, stride=1, stride_axis=0)
        at = pl.multiple_of((127 - q) * 128, 128)
        toep[pl.ds(at, 128), :] = jnp.where(keep, now, before).astype(bf16)
        return now

    lax.fori_loop(0, 128, toeplitz, jnp.zeros((128, 128), f32))

    col_arrive(yr, y_sem)
    lhs[:128, :] = jnp.zeros((128, 2048), bf16)
    seq = yr[...].reshape(256, ROWS)
    for b in range(16):
        lhs[128:, b * 128 : (b + 1) * 128] = jnp.dot(
            sel[b * 128 : (b + 1) * 128, :], seq, preferred_element_type=f32
        ).astype(bf16)
    acc[...] = jnp.zeros_like(acc)

    @pl.loop(0, 8)
    def _(k):
        r0 = pl.multiple_of(14464 - k * 2048, 128)
        r1 = pl.multiple_of(14336 - k * 2048, 128)
        left = lhs[pl.ds(pl.multiple_of(128 - k * 16, 16), 128), :]
        right = jnp.concatenate([toep[pl.ds(r0, 2048), :], toep[pl.ds(r1, 2048), :]], axis=1)
        acc[...] += jnp.dot(left, right, preferred_element_type=f32)

    ys2[...] = acc[...].astype(bf16).reshape(NY, 16, 256)
    col_exchange(lambda p: ys2.at[p], yr2, y2_sem)
    yr2[y] = ys2[y]
    col_arrive(yr2, y2_sem)
    back = jnp.dot(
        perm2[...], yr2[...].reshape(128, 256), preferred_element_type=f32
    ).astype(bf16)
    for b in range(8):
        for par in range(2):
            xs2[2 * b + par] = back[16 * b : 16 * b + 16, 128 * par : 128 * par + 128]
    row_exchange(xs2, xr2, x2_sem)
    xr2[xc] = xs2[xc]
    copies[3].wait()
    row_arrive(xr2, x2_sem)
    conv = xr2[...].reshape(CHAN, ROWS).astype(f32).T
    hid[z] = (query_v[...] * (conv + skip_v[...] * gated_v[...])).astype(bf16)

    copies[4].wait()
    half = ROWS // 2

    def zcopy(step, part, sems, to):
        b = (z + NZ - step) % NZ if sems is zr_sem else (z + step) % NZ
        at = hid.at[b, pl.ds(part * half, half)]
        return send(at, at, sems, step * 2 + part, step * 2 + part, ctx, to)

    def arrived(step, part, sems):
        b = (z + NZ - step - 1) % NZ if sems is zr_sem else (z + step + 1) % NZ
        at = hid.at[b, pl.ds(part * half, half)]
        send(at, at, sems, step * 2 + part, step * 2 + part, ctx, z).wait_recv()

    def out_part(b):
        at = pl.ds(pl.multiple_of(b * CHAN, CHAN), CHAN)
        return jnp.dot(hid[b], ob[at, :], preferred_element_type=f32)

    for part in range(2):
        go(zcopy(0, part, zr_sem, zp))
        go(zcopy(0, part, zl_sem, zm))
    oacc[...] = out_part(z)
    for step in range(3):
        for part in range(2):
            arrived(step, part, zr_sem)
            if step < 2 or part == 0:
                go(zcopy(step + 1, part, zr_sem, zp))
            arrived(step, part, zl_sem)
            if step < 2 or part == 1:
                go(zcopy(step + 1, part, zl_sem, zm))
        oacc[...] += out_part((z + NZ - step - 1) % NZ)
        oacc[...] += out_part((z + step + 1) % NZ)
    arrived(3, 0, zr_sem)
    arrived(3, 1, zl_sem)
    out_ref[...] = (oacc[...] + out_part((z + 4) % NZ)).astype(bf16)
    for copy in sent:
        copy.wait_send()


def per_device(hidden_in, in_proj, short_taps, long_filters, skip_gain, out_proj):
    f32, bf16 = jnp.float32, jnp.bfloat16
    VMEM, DMA = pltpu.VMEM, pltpu.SemaphoreType.DMA
    scratch = [
        VMEM((ROWS, MODEL), bf16),
        VMEM((3, MODEL, CHAN), bf16),
        VMEM((NZ * CHAN, FEATS), bf16),
        VMEM((3, 3, CHAN), bf16),
        VMEM((NX, ROWS), f32),
        VMEM((1, CHAN), f32),
        VMEM((3, ROWS, CHAN), f32),
        VMEM((3, 8, CHAN), bf16),
        VMEM((3, 8, CHAN), bf16),
        VMEM((3, ROWS + 8, CHAN), f32),
        VMEM((ROWS, CHAN), f32),
        VMEM((ROWS, CHAN), f32),
        VMEM((NX, 1, ROWS), f32),
        VMEM((NX, 1, ROWS), f32),
        VMEM((NX, ROWS), f32),
        VMEM((NY, NX, ROWS), f32),
        VMEM((TOEP, 128), bf16),
        VMEM((256, 256), bf16),
        VMEM((128, 128), bf16),
        VMEM((2048, 256), bf16),
        VMEM((256, 2048), bf16),
        VMEM((NX, 16, ROWS), bf16),
        VMEM((NX, 16, ROWS), bf16),
        VMEM((NY, 32, ROWS), bf16),
        VMEM((NY, 32, ROWS), bf16),
        VMEM((128, 256), f32),
        VMEM((NY, 16, 256), bf16),
        VMEM((NY, 16, 256), bf16),
        VMEM((NX, 16, ROWS), bf16),
        VMEM((NX, 16, ROWS), bf16),
        VMEM((NZ, ROWS, CHAN), bf16),
        VMEM((ROWS, FEATS), f32),
        DMA((5,)),
        DMA((3, NK)),
        DMA((2, 3)),
        DMA((2, NX)),
        DMA((2, NY)),
        DMA((2, NX)),
        DMA((2, NY)),
        DMA((2, NY)),
        DMA((2, NX)),
        DMA((2, 8)),
        DMA((2, 8)),
    ]
    return pl.pallas_call(
        kernel,
        out_shape=jax.ShapeDtypeStruct((ROWS, FEATS), bf16),
        in_specs=[pl.BlockSpec(memory_space=pl.ANY)] * 6,
        out_specs=pl.BlockSpec(memory_space=pltpu.VMEM),
        scratch_shapes=scratch,
        compiler_params=pltpu.CompilerParams(
            collective_id=0, has_side_effects=True, vmem_limit_bytes=48 * 1024 * 1024
        ),
    )(
        hidden_in,
        jnp.transpose(in_proj, (1, 0, 2)),
        short_taps,
        long_filters.T,
        skip_gain.reshape(1, CHAN),
        out_proj,
    )


def solution(mesh):
    in_specs = (
        P("ctx", None),
        P(None, None, "tp"),
        P(None, None, "tp"),
        P("ctx", "tp"),
        P("tp"),
        P(None, "tp"),
    )
    return jax.shard_map(
        per_device, mesh=mesh, in_specs=in_specs, out_specs=P("ctx", "tp"), check_vma=False
    )
```

```python
import functools

import jax
import jax.numpy as jnp
from jax import lax
from jax.experimental import pallas as pl
from jax.experimental.pallas import tpu as pltpu
from jax.sharding import PartitionSpec as P

MESH = pl.DeviceIdType.MESH
NX = 16
NY = 8
NZ = 8
ROWS = 128
CHAN = 256
MODEL = 4096
FEATS = 512
KCH = 1024
NK = MODEL // KCH
TOEP = 16512


def kernel(
    x_hbm, w_hbm, taps_hbm, filt_hbm, skip_hbm, o_hbm, out_ref,
    xb, wb, ob, taps_v, filt_v, skip_v,
    pacc, halo_s, halo_r, ext, query_t, direct_t,
    fs, fr, hs, hr, toep, perm1, perm2, lhs,
    xs, xr, ys, yr, acc, ys2, yr2, xs2, xr2, hid, oacc,
    in_sem, w_sem, o_sem, halo_sem, f_sem, h_sem, x_sem, y_sem, y2_sem, x2_sem, zr_sem, zl_sem,
):
    f32, bf16 = jnp.float32, jnp.bfloat16
    ctx = lax.axis_index("ctx")
    z = lax.axis_index("tp")
    y, xc = ctx // NX, ctx % NX
    x, core = xc // 2, xc % 2
    nxt, prv = (ctx + 1) % (NX * NY), (ctx + NX * NY - 1) % (NX * NY)
    zp, zm = (z + 1) % NZ, (z + NZ - 1) % NZ

    away = (0, 1, -1, 2, -2, 3, -3, 4)
    slot_of = {(dx, dc): 2 * k + dc for k, dx in enumerate(away) for dc in range(2)}
    back_of = {(dx, dc): slot_of[(4 if dx == 4 else -dx, dc)] for dx, dc in slot_of}
    row_peers = [key for key in slot_of if key != (0, 0)]
    far_first = row_peers[::-1]

    def rowpeer(key):
        return (x + key[0] + 8) % 8 * 2 + (core + key[1]) % 2

    def colpeer(o):
        return (y + o) % NY

    copies = [
        pltpu.make_async_copy(x_hbm, xb, in_sem.at[0]),
        pltpu.make_async_copy(taps_hbm, taps_v, in_sem.at[1]),
        pltpu.make_async_copy(filt_hbm, filt_v, in_sem.at[2]),
        pltpu.make_async_copy(skip_hbm, skip_v, in_sem.at[3]),
    ]

    def wcopy(j, c):
        at = pl.ds(c * KCH, KCH)
        return pltpu.make_async_copy(w_hbm.at[j, at], wb.at[j, at], w_sem.at[j, c])

    def ocopy(key):
        k = slot_of[key]
        return pltpu.make_async_copy(o_hbm.at[:, rowpeer(key)], ob.at[:, k], o_sem.at[k])

    copies[0].start()
    for j in (1, 2):
        for c in range(NK):
            wcopy(j, c).start()
    copies[2].start()
    copies[1].start()
    copies[3].start()

    barrier = pltpu.get_barrier_semaphore()
    for key in far_first:
        pl.semaphore_signal(barrier, inc=1, device_id=(y * NX + rowpeer(key), z), device_id_type=MESH)
    for o in (4, 3, 5, 2, 6, 1, 7):
        pl.semaphore_signal(barrier, inc=1, device_id=(colpeer(o) * NX + xc, z), device_id_type=MESH)
    for peer in ((ctx, zp), (ctx, zm), (nxt, z), (prv, z)):
        pl.semaphore_signal(barrier, inc=1, device_id=peer, device_id_type=MESH)

    row = lax.broadcasted_iota(jnp.int32, (256, 256), 0)
    col = lax.broadcasted_iota(jnp.int32, (256, 256), 1)
    take = (row % 16 // 2 * 2 + row // 16 % 2) * 16 + row // 32 * 2 + row % 2
    perm1[...] = jnp.where(col == take, 1.0, 0.0).astype(bf16)
    row = lax.broadcasted_iota(jnp.int32, (128, 128), 0)
    col = lax.broadcasted_iota(jnp.int32, (128, 128), 1)
    perm2[...] = jnp.where(col == (row % 16 // 2) * 16 + row // 16 * 2 + row % 2, 1.0, 0.0).astype(bf16)
    pacc[...] = jnp.zeros_like(pacc)
    acc[...] = jnp.zeros_like(acc)
    for k in range(1, 8):
        lhs[: 16 * k, k * 256 : (k + 1) * 256] = jnp.zeros((16 * k, 256), bf16)
    toep[128 * 128 :, :] = jnp.zeros((128, 128), bf16)

    def send(src, dst, sems, k_send, k_recv, c, t):
        return pltpu.make_async_remote_copy(
            src_ref=src, dst_ref=dst, send_sem=sems.at[0, k_send], recv_sem=sems.at[1, k_recv],
            device_id=(c, t), device_id_type=MESH)

    sent = []

    def go(copy):
        copy.start()
        sent.append(copy)

    def row_exchange(src, dst_of, sems):
        for key in far_first:
            p = rowpeer(key)
            go(send(src.at[p], dst_of(key), sems, slot_of[key], back_of[key], y * NX + p, z))

    def row_arrive(dst, sems):
        for key in row_peers:
            at = dst.at[rowpeer(key)]
            send(at, at, sems, slot_of[key], slot_of[key], ctx, z).wait_recv()

    def col_exchange(src_of, dst, sems):
        for o in (4, 3, 5, 2, 6, 1, 7):
            p = colpeer(o)
            go(send(src_of(p), dst.at[y], sems, o, o, p * NX + xc, z))

    def col_wait(p, dst, sems):
        o = (y + NY - p) % NY
        send(dst.at[p], dst.at[p], sems, o, o, ctx, z).wait_recv()

    def col_arrive(dst, sems):
        for o in (7, 1, 6, 2, 5, 3, 4):
            col_wait((y + NY - o) % NY, dst, sems)

    copies[0].wait()

    def project(j):
        @pl.loop(0, NK)
        def _(c):
            wcopy(j, c).wait()
            at = pl.ds(pl.multiple_of(c * KCH, KCH), KCH)
            pacc[j] += jnp.dot(xb[:, at], wb[j, at, :], preferred_element_type=f32)

        rounded = pacc[j].astype(bf16)
        ext[j, 8:, :] = rounded.astype(f32)
        halo_s[j] = rounded[ROWS - 8 :, :]

    def halo(j):
        return send(halo_s.at[j], halo_r.at[j], halo_sem, j, j, nxt, z)

    def short_conv(j):
        send(halo_r.at[j], halo_r.at[j], halo_sem, j, j, ctx, z).wait_recv()
        before = halo_r[j].astype(f32)
        ext[j, :8, :] = jnp.where(ctx == 0, jnp.zeros_like(before), before)
        taps = [taps_v[i].astype(f32)[j : j + 1, :] for i in range(3)]
        return (
            taps[0] * ext[j, 8:, :]
            + taps[1] * ext[j, 7 : 7 + ROWS, :]
            + taps[2] * ext[j, 6 : 6 + ROWS, :]
        )

    project(1)
    project(2)
    for c in range(NK):
        wcopy(0, c).start()
    pl.semaphore_wait(barrier, NX - 1 + NY - 1 + 4)
    go(halo(1))
    go(halo(2))

    copies[2].wait()
    for f in range(NX):
        fs[f] = filt_v[f : f + 1, :]
    row_exchange(fs, lambda key: fr.at[xc], f_sem)
    fr[xc] = fs[xc]
    copies[1].wait()
    copies[3].wait()
    keyed = short_conv(1)
    gated = keyed * short_conv(2)
    xs[...] = gated.T.astype(bf16).reshape(NX, 16, ROWS)
    row_exchange(xs, lambda key: xr.at[xc], x_sem)
    xr[xc] = xs[xc]
    direct_t[...] = (skip_v[...] * gated).T
    for key in slot_of:
        ocopy(key).start()

    project(0)
    go(halo(0))

    row_arrive(fr, f_sem)
    hs[...] = fr[...].reshape(NX, ROWS)
    col_exchange(lambda p: hs, hr, h_sem)
    hr[y] = hs[...]

    row_arrive(xr, x_sem)
    ys[...] = jnp.dot(
        perm1[...], xr[...].reshape(256, ROWS), preferred_element_type=f32
    ).astype(bf16).reshape(NY, 2, 16, ROWS)
    col_exchange(lambda p: ys.at[p], yr, y_sem)
    yr[y] = ys[y]

    lane = lax.broadcasted_iota(jnp.int32, (128, 128), 1)
    sub = lax.broadcasted_iota(jnp.int32, (128, 128), 0)
    keep = lane >= sub

    def toeplitz(p, before):
        @pl.when(p != y)
        def _():
            col_wait(p, hr, h_sem)

        for j in range(16):
            line = hr[p, j : j + 1, :]
            now = pltpu.roll(jnp.broadcast_to(line, (128, 128)), 0, 1, stride=1, stride_axis=0)
            at = pl.multiple_of((127 - j) * 128 - p * 2048, 128)
            toep[pl.ds(at, 128), :] = jnp.where(keep, now, before).astype(bf16)
            before = now
        return before

    lax.fori_loop(0, NY, toeplitz, jnp.zeros((128, 128), f32))

    col_arrive(yr, y_sem)
    for k in range(8):
        for p in range(8 - k):
            for par in range(2):
                at = k * 256 + par * 128
                lhs[16 * (p + k) : 16 * (p + k + 1), at : at + 128] = yr[p, par]

    @pl.loop(0, 8)
    def _(i):
        right = []
        for k in range(8):
            r0 = pl.multiple_of(14464 - 2048 * k + 256 * i, 128)
            r1 = pl.multiple_of(14336 - 2048 * k + 256 * i, 128)
            right.append(jnp.concatenate([toep[pl.ds(r0, 256), :], toep[pl.ds(r1, 256), :]], axis=1))
        acc[8:, :] = acc[6 : 6 + 128, :] + jnp.dot(
            lhs[...], jnp.concatenate(right, axis=0), preferred_element_type=f32
        )

    ys2[...] = acc[8:, :].astype(bf16).reshape(NY, 16, 256)
    col_exchange(lambda p: ys2.at[p], yr2, y2_sem)
    yr2[y] = ys2[y]
    query_t[...] = short_conv(0).T
    for key in slot_of:
        ocopy(key).wait()
    col_arrive(yr2, y2_sem)
    back = jnp.dot(
        perm2[...], yr2[...].reshape(128, 256), preferred_element_type=f32
    ).astype(bf16)
    for b in range(8):
        for par in range(2):
            xs2[2 * b + par] = back[16 * b : 16 * b + 16, 128 * par : 128 * par + 128]
    row_exchange(xs2, lambda key: xr2.at[back_of[key]], x2_sem)
    xr2[0] = xs2[xc]

    def own(g):
        for k in range(4 * g, 4 * g + 4):
            key = (away[k // 2], k % 2)
            if key != (0, 0):
                send(xr2.at[k], xr2.at[k], x2_sem, k, k, ctx, z).wait_recv()
            at = pl.ds(pl.multiple_of(rowpeer(key) * 16, 16), 16)
            hid[z, k] = (query_t[at, :] * (xr2[k].astype(f32) + direct_t[at, :])).astype(bf16)
        forward(0, g)

    def part(b, g):
        return hid.at[b, pl.ds(4 * g, 4)]

    def forward(d, g):
        if d < 3 or g % 2 == 0:
            at = part((z + NZ - d) % NZ, g)
            go(send(at, at, zr_sem, 4 * d + g, 4 * d + g, ctx, zp))
        if d < 3 or g % 2 == 1:
            at = part((z + d) % NZ, g)
            go(send(at, at, zl_sem, 4 * d + g, 4 * d + g, ctx, zm))

    def arrive(d, g):
        k = 4 * (d - 1) + g
        if d < 4 or g % 2 == 0:
            at = part((z + NZ - d) % NZ, g)
            send(at, at, zr_sem, k, k, ctx, z).wait_recv()
        if d < 4 or g % 2 == 1:
            at = part((z + d) % NZ, g)
            send(at, at, zl_sem, k, k, ctx, z).wait_recv()
        if d < 4:
            forward(d, g)

    def out_part(b):
        return lax.dot_general(
            hid[b].reshape(CHAN, ROWS), ob[b].reshape(CHAN, FEATS),
            (((0,), (0,)), ((), ())), preferred_element_type=f32)

    ready, hop = (1.2, 2.5, 3.7, 5.0), 1.9
    events = sorted((ready[g] + hop * d, d, g) for d in range(5) for g in range(4))
    for _, d, g in events:
        if d == 0:
            own(g)
        else:
            arrive(d, g)
        if g == 3:
            if d == 0:
                oacc[...] = out_part(z)
            elif d < 4:
                oacc[...] += out_part((z + NZ - d) % NZ) + out_part((z + d) % NZ)
    out_ref[...] = (oacc[...] + out_part((z + 4) % NZ)).astype(bf16)
    for copy in sent:
        copy.wait_send()


def per_device(hidden_in, in_proj, short_taps, long_filters, skip_gain, out_proj):
    f32, bf16 = jnp.float32, jnp.bfloat16
    VMEM, DMA = pltpu.VMEM, pltpu.SemaphoreType.DMA
    scratch = [
        VMEM((ROWS, MODEL), bf16),
        VMEM((3, MODEL, CHAN), bf16),
        VMEM((NZ, NX, 16, FEATS), bf16),
        VMEM((3, 3, CHAN), bf16),
        VMEM((NX, ROWS), f32),
        VMEM((1, CHAN), f32),
        VMEM((3, ROWS, CHAN), f32),
        VMEM((3, 8, CHAN), bf16),
        VMEM((3, 8, CHAN), bf16),
        VMEM((3, ROWS + 8, CHAN), f32),
        VMEM((CHAN, ROWS), f32),
        VMEM((CHAN, ROWS), f32),
        VMEM((NX, 1, ROWS), f32),
        VMEM((NX, 1, ROWS), f32),
        VMEM((NX, ROWS), f32),
        VMEM((NY, NX, ROWS), f32),
        VMEM((TOEP, 128), bf16),
        VMEM((256, 256), bf16),
        VMEM((128, 128), bf16),
        VMEM((128, 2048), bf16),
        VMEM((NX, 16, ROWS), bf16),
        VMEM((NX, 16, ROWS), bf16),
        VMEM((NY, 2, 16, ROWS), bf16),
        VMEM((NY, 2, 16, ROWS), bf16),
        VMEM((136, 256), f32),
        VMEM((NY, 16, 256), bf16),
        VMEM((NY, 16, 256), bf16),
        VMEM((NX, 16, ROWS), bf16),
        VMEM((NX, 16, ROWS), bf16),
        VMEM((NZ, NX, 16, ROWS), bf16),
        VMEM((ROWS, FEATS), f32),
        DMA((4,)),
        DMA((3, NK)),
        DMA((NX,)),
        DMA((2, 3)),
        DMA((2, NX)),
        DMA((2, NY)),
        DMA((2, NX)),
        DMA((2, NY)),
        DMA((2, NY)),
        DMA((2, NX)),
        DMA((2, 16)),
        DMA((2, 16)),
    ]
    return pl.pallas_call(
        kernel,
        out_shape=jax.ShapeDtypeStruct((ROWS, FEATS), bf16),
        in_specs=[pl.BlockSpec(memory_space=pl.ANY)] * 6,
        out_specs=pl.BlockSpec(memory_space=pltpu.VMEM),
        scratch_shapes=scratch,
        compiler_params=pltpu.CompilerParams(
            collective_id=0, has_side_effects=True, vmem_limit_bytes=67043328
        ),
    )(
        hidden_in,
        jnp.transpose(in_proj, (1, 0, 2)),
        short_taps,
        long_filters.T,
        skip_gain.reshape(1, CHAN),
        out_proj.reshape(NZ, NX, 16, FEATS),
    )


def solution(mesh):
    in_specs = (
        P("ctx", None),
        P(None, None, "tp"),
        P(None, None, "tp"),
        P("ctx", "tp"),
        P("tp"),
        P(None, "tp"),
    )
    return jax.shard_map(
        per_device, mesh=mesh, in_specs=in_specs, out_specs=P("ctx", "tp"), check_vma=False
    )
```

```python
import functools

import jax
import jax.numpy as jnp
from jax import lax
from jax.experimental import pallas as pl
from jax.experimental.pallas import tpu as pltpu
from jax.sharding import PartitionSpec as P

MESH = pl.DeviceIdType.MESH
NX = 16
NY = 8
NZ = 8
ROWS = 128
CHAN = 256
MODEL = 4096
FEATS = 512
KCH = 1024
NK = MODEL // KCH
TOEP = 16512


def kernel(
    x_hbm, w_hbm, taps_hbm, filt_hbm, skip_hbm, o_hbm, out_ref,
    xb, wb, ob, taps_v, filt_v, skip_v,
    pacc, halo_s, halo_r, ext, query_t, direct_t,
    fs, fr, hs, hr, toep, perm1, perm2, lhs,
    xs, xr, ys, yr, acc, ys2, yr2, xs2, xr2, hid, oacc,
    in_sem, w_sem, o_sem, halo_sem, f_sem, h_sem, x_sem, y_sem, y2_sem, x2_sem, z_sem,
):
    f32, bf16 = jnp.float32, jnp.bfloat16
    ctx = lax.axis_index("ctx")
    z = lax.axis_index("tp")
    y, xc = ctx // NX, ctx % NX
    x, core = xc // 2, xc % 2
    nxt, prv = (ctx + 1) % (NX * NY), (ctx + NX * NY - 1) % (NX * NY)
    zm = (z + NZ - 1) % NZ

    away = (0, 1, -1, 2, -2, 3, -3, 4)
    slot_of = {(dx, dc): 2 * k + dc for k, dx in enumerate(away) for dc in range(2)}
    back_of = {(dx, dc): slot_of[(4 if dx == 4 else -dx, dc)] for dx, dc in slot_of}
    row_peers = [key for key in slot_of if key != (0, 0)]
    far_first = row_peers[::-1]

    def rowpeer(key):
        return (x + key[0] + 8) % 8 * 2 + (core + key[1]) % 2

    def colpeer(o):
        return (y + o) % NY

    copies = [
        pltpu.make_async_copy(x_hbm, xb, in_sem.at[0]),
        pltpu.make_async_copy(taps_hbm, taps_v, in_sem.at[1]),
        pltpu.make_async_copy(filt_hbm, filt_v, in_sem.at[2]),
        pltpu.make_async_copy(skip_hbm, skip_v, in_sem.at[3]),
    ]

    def wcopy(j, c):
        at = pl.ds(c * KCH, KCH)
        return pltpu.make_async_copy(w_hbm.at[j, at], wb.at[j, at], w_sem.at[j, c])

    def ocopy(key):
        k = slot_of[key]
        return pltpu.make_async_copy(o_hbm.at[:, rowpeer(key)], ob.at[k // 4, :, k % 4], o_sem.at[k])

    copies[0].start()
    for j in (1, 2):
        for c in range(NK):
            wcopy(j, c).start()
    copies[2].start()
    copies[1].start()
    copies[3].start()

    barrier = pltpu.get_barrier_semaphore()
    for key in far_first:
        pl.semaphore_signal(barrier, inc=1, device_id=(y * NX + rowpeer(key), z), device_id_type=MESH)
    for o in (4, 3, 5, 2, 6, 1, 7):
        pl.semaphore_signal(barrier, inc=1, device_id=(colpeer(o) * NX + xc, z), device_id_type=MESH)
    for peer in ((nxt, z), (prv, z)):
        pl.semaphore_signal(barrier, inc=1, device_id=peer, device_id_type=MESH)
    for o in (4, 3, 5, 2, 6, 1, 7):
        pl.semaphore_signal(barrier, inc=1, device_id=(ctx, (z + o) % NZ), device_id_type=MESH)

    row = lax.broadcasted_iota(jnp.int32, (256, 256), 0)
    col = lax.broadcasted_iota(jnp.int32, (256, 256), 1)
    take = (row % 16 // 2 * 2 + row // 16 % 2) * 16 + row // 32 * 2 + row % 2
    perm1[...] = jnp.where(col == take, 1.0, 0.0).astype(bf16)
    row = lax.broadcasted_iota(jnp.int32, (128, 128), 0)
    col = lax.broadcasted_iota(jnp.int32, (128, 128), 1)
    perm2[...] = jnp.where(col == (row % 16 // 2) * 16 + row // 16 * 2 + row % 2, 1.0, 0.0).astype(bf16)
    pacc[...] = jnp.zeros_like(pacc)
    acc[...] = jnp.zeros_like(acc)
    for k in range(1, 8):
        lhs[: 16 * k, k * 256 : (k + 1) * 256] = jnp.zeros((16 * k, 256), bf16)
    toep[128 * 128 :, :] = jnp.zeros((128, 128), bf16)

    def send(src, dst, sems, k_send, k_recv, c, t):
        return pltpu.make_async_remote_copy(
            src_ref=src, dst_ref=dst, send_sem=sems.at[0, k_send], recv_sem=sems.at[1, k_recv],
            device_id=(c, t), device_id_type=MESH)

    sent = []

    def go(copy):
        copy.start()
        sent.append(copy)

    def row_exchange(src, dst_of, sems):
        for key in far_first:
            p = rowpeer(key)
            go(send(src.at[p], dst_of(key), sems, slot_of[key], back_of[key], y * NX + p, z))

    def row_arrive(dst, sems):
        for key in row_peers:
            at = dst.at[rowpeer(key)]
            send(at, at, sems, slot_of[key], slot_of[key], ctx, z).wait_recv()

    def col_exchange(src_of, dst, sems):
        for o in (4, 3, 5, 2, 6, 1, 7):
            p = colpeer(o)
            go(send(src_of(p), dst.at[y], sems, o, o, p * NX + xc, z))

    def col_wait(p, dst, sems):
        o = (y + NY - p) % NY
        send(dst.at[p], dst.at[p], sems, o, o, ctx, z).wait_recv()

    def col_arrive(dst, sems):
        for o in (7, 1, 6, 2, 5, 3, 4):
            col_wait((y + NY - o) % NY, dst, sems)

    copies[0].wait()

    def project(j):
        @pl.loop(0, NK)
        def _(c):
            wcopy(j, c).wait()
            at = pl.ds(pl.multiple_of(c * KCH, KCH), KCH)
            pacc[j] += jnp.dot(xb[:, at], wb[j, at, :], preferred_element_type=f32)

        rounded = pacc[j].astype(bf16)
        ext[j, 8:, :] = rounded.astype(f32)
        halo_s[j] = rounded[ROWS - 8 :, :]

    def halo(j):
        return send(halo_s.at[j], halo_r.at[j], halo_sem, j, j, nxt, z)

    def short_conv(j):
        send(halo_r.at[j], halo_r.at[j], halo_sem, j, j, ctx, z).wait_recv()
        before = halo_r[j].astype(f32)
        ext[j, :8, :] = jnp.where(ctx == 0, jnp.zeros_like(before), before)
        taps = [taps_v[i].astype(f32)[j : j + 1, :] for i in range(3)]
        return (
            taps[0] * ext[j, 8:, :]
            + taps[1] * ext[j, 7 : 7 + ROWS, :]
            + taps[2] * ext[j, 6 : 6 + ROWS, :]
        )

    copies[2].wait()
    for f in range(NX):
        fs[f] = filt_v[f : f + 1, :]
    project(1)
    project(2)
    for c in range(NK):
        wcopy(0, c).start()
    pl.semaphore_wait(barrier, NX - 1 + NY - 1 + 2 + NZ - 1)
    go(halo(1))
    go(halo(2))

    row_exchange(fs, lambda key: fr.at[xc], f_sem)
    fr[xc] = fs[xc]
    copies[1].wait()
    copies[3].wait()
    keyed = short_conv(1)
    gated = keyed * short_conv(2)
    xs[...] = gated.T.astype(bf16).reshape(NX, 16, ROWS)
    row_exchange(xs, lambda key: xr.at[xc], x_sem)
    xr[xc] = xs[xc]

    row_arrive(fr, f_sem)
    hs[...] = fr[...].reshape(NX, ROWS)
    col_exchange(lambda p: hs, hr, h_sem)
    hr[y] = hs[...]

    project(0)
    go(halo(0))
    direct_t[...] = (skip_v[...] * gated).T

    row_arrive(xr, x_sem)
    ys[...] = jnp.dot(
        perm1[...], xr[...].reshape(256, ROWS), preferred_element_type=f32
    ).astype(bf16).reshape(NY, 2, 16, ROWS)
    col_exchange(lambda p: ys.at[p], yr, y_sem)
    yr[y] = ys[y]
    for key in slot_of:
        ocopy(key).start()

    lane = lax.broadcasted_iota(jnp.int32, (128, 128), 1)
    sub = lax.broadcasted_iota(jnp.int32, (128, 128), 0)
    keep = lane >= sub

    def toeplitz(p, before):
        @pl.when(p != y)
        def _():
            col_wait(p, hr, h_sem)

        for j in range(16):
            line = hr[p, j : j + 1, :]
            now = pltpu.roll(jnp.broadcast_to(line, (128, 128)), 0, 1, stride=1, stride_axis=0)
            at = pl.multiple_of((127 - j) * 128 - p * 2048, 128)
            toep[pl.ds(at, 128), :] = jnp.where(keep, now, before).astype(bf16)
            before = now
        return before

    lax.fori_loop(0, NY, toeplitz, jnp.zeros((128, 128), f32))

    col_arrive(yr, y_sem)
    for k in range(8):
        for p in range(8 - k):
            for par in range(2):
                at = k * 256 + par * 128
                lhs[16 * (p + k) : 16 * (p + k + 1), at : at + 128] = yr[p, par]

    @pl.loop(0, 8)
    def _(i):
        right = []
        for k in range(8):
            r0 = pl.multiple_of(14464 - 2048 * k + 256 * i, 128)
            r1 = pl.multiple_of(14336 - 2048 * k + 256 * i, 128)
            right.append(jnp.concatenate([toep[pl.ds(r0, 256), :], toep[pl.ds(r1, 256), :]], axis=1))
        acc[8:, :] = acc[6 : 6 + 128, :] + jnp.dot(
            lhs[...], jnp.concatenate(right, axis=0), preferred_element_type=f32
        )

    ys2[...] = acc[8:, :].astype(bf16).reshape(NY, 16, 256)
    col_exchange(lambda p: ys2.at[p], yr2, y2_sem)
    yr2[y] = ys2[y]
    query_t[...] = short_conv(0).T
    for key in slot_of:
        ocopy(key).wait()
    while sent:
        sent.pop(0).wait_send()
    col_arrive(yr2, y2_sem)
    back = jnp.dot(
        perm2[...], yr2[...].reshape(128, 256), preferred_element_type=f32
    ).astype(bf16)
    for b in range(8):
        for par in range(2):
            xs2[2 * b + par] = back[16 * b : 16 * b + 16, 128 * par : 128 * par + 128]
    row_exchange(xs2, lambda key: xr2.at[back_of[key]], x2_sem)
    xr2[0] = xs2[xc]

    def block(g, o):
        return hid.at[g, (z + o) % NZ]

    def zsend(g, o_block, o_to):
        at = block(g, o_block)
        k = (o_block - o_to) % NZ
        return send(at, at, z_sem, g * NZ + o_to, g * NZ + k, ctx, (z + o_to) % NZ)

    def arrive(g, o):
        at = block(g, o)
        send(at, at, z_sem, g * NZ + o, g * NZ + o, ctx, z).wait_recv()

    relayed = (0, 1)

    def own(g):
        for k in range(4 * g, 4 * g + 4):
            key = (away[k // 2], k % 2)
            if key != (0, 0):
                send(xr2.at[k], xr2.at[k], x2_sem, k, k, ctx, z).wait_recv()
            at = pl.ds(pl.multiple_of(rowpeer(key) * 16, 16), 16)
            hid[g, z, k - 4 * g] = (query_t[at, :] * (xr2[k].astype(f32) + direct_t[at, :])).astype(bf16)
        for o in (4, 3, 5, 2, 6, 1, 7):
            if o != 4 or g not in relayed:
                go(zsend(g, 0, o))

    def relay(g):
        arrive(g, 3)
        at = block(g, 3)
        go(send(at, at, z_sem, g * NZ + 4, g * NZ + 4, ctx, zm))

    def out_part(g):
        for o in (1, 7, 2, 6, 3, 5, 4):
            if o != 3 or g not in relayed:
                arrive(g, o)
        return lax.dot_general(
            hid[g].reshape(NZ * 64, ROWS), ob[g].reshape(NZ * 64, FEATS),
            (((0,), (0,)), ((), ())), preferred_element_type=f32)

    for g in range(4):
        own(g)
    for g in relayed:
        relay(g)
    oacc[...] = out_part(0)
    oacc[...] += out_part(1)
    oacc[...] += out_part(2)
    out_ref[...] = (oacc[...] + out_part(3)).astype(bf16)
    for copy in sent:
        copy.wait_send()


def per_device(hidden_in, in_proj, short_taps, long_filters, skip_gain, out_proj):
    f32, bf16 = jnp.float32, jnp.bfloat16
    VMEM, DMA = pltpu.VMEM, pltpu.SemaphoreType.DMA
    scratch = [
        VMEM((ROWS, MODEL), bf16),
        VMEM((3, MODEL, CHAN), bf16),
        VMEM((4, NZ, 4, 16, FEATS), bf16),
        VMEM((3, 3, CHAN), bf16),
        VMEM((NX, ROWS), f32),
        VMEM((1, CHAN), f32),
        VMEM((3, ROWS, CHAN), f32),
        VMEM((3, 8, CHAN), bf16),
        VMEM((3, 8, CHAN), bf16),
        VMEM((3, ROWS + 8, CHAN), f32),
        VMEM((CHAN, ROWS), f32),
        VMEM((CHAN, ROWS), f32),
        VMEM((NX, 1, ROWS), f32),
        VMEM((NX, 1, ROWS), f32),
        VMEM((NX, ROWS), f32),
        VMEM((NY, NX, ROWS), f32),
        VMEM((TOEP, 128), bf16),
        VMEM((256, 256), bf16),
        VMEM((128, 128), bf16),
        VMEM((128, 2048), bf16),
        VMEM((NX, 16, ROWS), bf16),
        VMEM((NX, 16, ROWS), bf16),
        VMEM((NY, 2, 16, ROWS), bf16),
        VMEM((NY, 2, 16, ROWS), bf16),
        VMEM((136, 256), f32),
        VMEM((NY, 16, 256), bf16),
        VMEM((NY, 16, 256), bf16),
        VMEM((NX, 16, ROWS), bf16),
        VMEM((NX, 16, ROWS), bf16),
        VMEM((4, NZ, 4, 16, ROWS), bf16),
        VMEM((ROWS, FEATS), f32),
        DMA((4,)),
        DMA((3, NK)),
        DMA((NX,)),
        DMA((2, 3)),
        DMA((2, NX)),
        DMA((2, NY)),
        DMA((2, NX)),
        DMA((2, NY)),
        DMA((2, NY)),
        DMA((2, NX)),
        DMA((2, 4 * NZ)),
    ]
    return pl.pallas_call(
        kernel,
        out_shape=jax.ShapeDtypeStruct((ROWS, FEATS), bf16),
        in_specs=[pl.BlockSpec(memory_space=pl.ANY)] * 6,
        out_specs=pl.BlockSpec(memory_space=pltpu.VMEM),
        scratch_shapes=scratch,
        compiler_params=pltpu.CompilerParams(
            collective_id=0, has_side_effects=True, vmem_limit_bytes=67043328
        ),
    )(
        hidden_in,
        jnp.transpose(in_proj, (1, 0, 2)),
        short_taps,
        long_filters.T,
        skip_gain.reshape(1, CHAN),
        out_proj.reshape(NZ, NX, 16, FEATS),
    )


def solution(mesh):
    in_specs = (
        P("ctx", None),
        P(None, None, "tp"),
        P(None, None, "tp"),
        P("ctx", "tp"),
        P("tp"),
        P(None, "tp"),
    )
    return jax.shard_map(
        per_device, mesh=mesh, in_specs=in_specs, out_specs=P("ctx", "tp"), check_vma=False
    )
```

```python
import functools

import jax
import jax.numpy as jnp
from jax import lax
from jax.experimental import pallas as pl
from jax.experimental.pallas import tpu as pltpu
from jax.sharding import PartitionSpec as P

MESH = pl.DeviceIdType.MESH
NX = 16
NY = 8
NZ = 8
ROWS = 128
CHAN = 256
MODEL = 4096
FEATS = 512
KCH = 1024
NK = MODEL // KCH
TOEP = 16512


def kernel(
    x_hbm, w_hbm, taps_hbm, filt_hbm, skip_hbm, o_hbm, out_ref,
    xb, wb, ob, taps_v, filt_v, skip_v,
    pacc, halo_s, halo_r, ext, query_t, direct_t,
    fs, fr, hs, hr, toep, perm1, perm2, lhs,
    xs, xr, ys, yr, acc, ys2, yr2, xs2, xr2, hid, oacc,
    in_sem, w_sem, o_sem, halo_sem, f_sem, h_sem, x_sem, y_sem, y2_sem, x2_sem, z_sem,
):
    f32, bf16 = jnp.float32, jnp.bfloat16
    ctx = lax.axis_index("ctx")
    z = lax.axis_index("tp")
    y, xc = ctx // NX, ctx % NX
    x, core = xc // 2, xc % 2
    nxt, prv = (ctx + 1) % (NX * NY), (ctx + NX * NY - 1) % (NX * NY)

    def chip(t):
        return 4 + (t + 1) // 2 * (1 - 2 * (t % 2))

    def rowpeer(e, dc):
        return (x + e) % 8 * 2 + (core + dc) % 2

    def row_loop(one):
        @pl.loop(0, 7)
        def _(t):
            one(chip(t), 0)
            one(chip(t), 1)

        one(0, 1)

    copies = [
        pltpu.make_async_copy(x_hbm, xb, in_sem.at[0]),
        pltpu.make_async_copy(taps_hbm, taps_v, in_sem.at[1]),
        pltpu.make_async_copy(filt_hbm, filt_v, in_sem.at[2]),
        pltpu.make_async_copy(skip_hbm, skip_v, in_sem.at[3]),
    ]

    def wcopy(j, c):
        at = pl.ds(c * KCH, KCH)
        return pltpu.make_async_copy(w_hbm.at[j, at], wb.at[j, at], w_sem.at[j, c])

    def ocopy(k):
        p = rowpeer(k // 2, k % 2)
        return pltpu.make_async_copy(o_hbm.at[:, p], ob.at[k // 4, :, k % 4], o_sem)

    copies[0].start()
    for j in (1, 2):
        for c in range(NK):
            wcopy(j, c).start()
    copies[2].start()
    copies[1].start()
    copies[3].start()

    barrier = pltpu.get_barrier_semaphore()

    def greet(c, t):
        pl.semaphore_signal(barrier, inc=1, device_id=(c, t), device_id_type=MESH)

    row_loop(lambda e, dc: greet(y * NX + rowpeer(e, dc), z))

    @pl.loop(1, 8)
    def _(o):
        greet((y + o) % NY * NX + xc, z)
        greet(ctx, (z + o) % NZ)

    greet(nxt, z)
    greet(prv, z)

    row = lax.broadcasted_iota(jnp.int32, (256, 256), 0)
    col = lax.broadcasted_iota(jnp.int32, (256, 256), 1)
    take = (row % 16 // 2 * 2 + row // 16 % 2) * 16 + row // 32 * 2 + row % 2
    perm1[...] = jnp.where(col == take, 1.0, 0.0).astype(bf16)
    row = lax.broadcasted_iota(jnp.int32, (128, 128), 0)
    col = lax.broadcasted_iota(jnp.int32, (128, 128), 1)
    perm2[...] = jnp.where(col == (row % 16 // 2) * 16 + row // 16 * 2 + row % 2, 1.0, 0.0).astype(bf16)
    pacc[...] = jnp.zeros_like(pacc)
    acc[...] = jnp.zeros_like(acc)
    for k in range(1, 8):
        lhs[: 16 * k, k * 256 : (k + 1) * 256] = jnp.zeros((16 * k, 256), bf16)
    toep[128 * 128 :, :] = jnp.zeros((128, 128), bf16)

    def send(src, dst, sems, c, t, k=1):
        return pltpu.make_async_remote_copy(
            src_ref=src, dst_ref=dst, send_sem=sems.at[0], recv_sem=sems.at[k],
            device_id=(c, t), device_id_type=MESH)

    def arrived(at, sems, k=1):
        send(at, at, sems, ctx, z, k).wait_recv()

    def left(at, sems):
        send(at, at, sems, ctx, z).wait_send()

    def row_exchange(src, dst, sems):
        def one(e, dc):
            p = rowpeer(e, dc)
            send(src.at[p], dst.at[xc], sems, y * NX + p, z).start()

        row_loop(one)

    def row_all(at):
        return at.at[pl.ds(0, NX - 1)]

    def col_exchange(src_of, dst, sems):
        @pl.loop(0, 7)
        def _(t):
            p = (y + chip(t)) % NY
            send(src_of(p), dst.at[y], sems, p * NX + xc, z).start()

    def col_all(at):
        return at.at[pl.ds(0, NY - 1)]

    copies[0].wait()

    def project(j, c):
        wcopy(j, c).wait()
        at = pl.ds(pl.multiple_of(c * KCH, KCH), KCH)
        pacc[j] += jnp.dot(xb[:, at], wb[j, at, :], preferred_element_type=f32)

    def projected(j):
        rounded = pacc[j].astype(bf16)
        ext[j, 8:, :] = rounded.astype(f32)
        halo_s[j] = rounded[ROWS - 8 :, :]

    kv, q = pl.ds(1, 2), pl.ds(0, 1)

    def short_conv(j):
        before = halo_r[j].astype(f32)
        ext[j, :8, :] = jnp.where(ctx == 0, jnp.zeros_like(before), before)
        taps = [taps_v[i].astype(f32)[j : j + 1, :] for i in range(3)]
        return (
            taps[0] * ext[j, 8:, :]
            + taps[1] * ext[j, 7 : 7 + ROWS, :]
            + taps[2] * ext[j, 6 : 6 + ROWS, :]
        )

    copies[2].wait()
    for f in range(NX):
        fs[f] = filt_v[f : f + 1, :]

    @pl.loop(0, 2 * NK)
    def _(i):
        project(1 + i // NK, i % NK)

    projected(1)
    projected(2)
    for c in range(NK):
        wcopy(0, c).start()
    pl.semaphore_wait(barrier, NX - 1 + NY - 1 + 2 + NZ - 1)
    send(halo_s.at[kv], halo_r.at[kv], halo_sem, nxt, z).start()

    row_exchange(fs, fr, f_sem)
    fr[xc] = fs[xc]
    copies[1].wait()
    copies[3].wait()
    arrived(halo_r.at[kv], halo_sem)
    keyed = short_conv(1)
    gated = keyed * short_conv(2)
    xs[...] = gated.T.astype(bf16).reshape(NX, 16, ROWS)
    row_exchange(xs, xr, x_sem)
    xr[xc] = xs[xc]

    arrived(row_all(fr), f_sem)
    hs[...] = fr[...].reshape(NX, ROWS)
    col_exchange(lambda p: hs, hr, h_sem)
    hr[y] = hs[...]

    @pl.loop(0, NK)
    def _(c):
        project(0, c)

    projected(0)
    send(halo_s.at[q], halo_r.at[q], halo_sem, nxt, z, 2).start()
    direct_t[...] = (skip_v[...] * gated).T

    arrived(row_all(xr), x_sem)
    ys[...] = jnp.dot(
        perm1[...], xr[...].reshape(256, ROWS), preferred_element_type=f32
    ).astype(bf16).reshape(NY, 2, 16, ROWS)
    col_exchange(lambda p: ys.at[p], yr, y_sem)
    yr[y] = ys[y]

    @pl.loop(0, NX)
    def _(k):
        ocopy(k).start()


    lane = lax.broadcasted_iota(jnp.int32, (128, 128), 1)
    sub = lax.broadcasted_iota(jnp.int32, (128, 128), 0)
    keep = lane >= sub

    arrived(col_all(hr), h_sem)

    def toeplitz(p, before):
        for j in range(16):
            line = hr[p, j : j + 1, :]
            now = pltpu.roll(jnp.broadcast_to(line, (128, 128)), 0, 1, stride=1, stride_axis=0)
            at = pl.multiple_of((127 - j) * 128 - p * 2048, 128)
            toep[pl.ds(at, 128), :] = jnp.where(keep, now, before).astype(bf16)
            before = now
        return before

    lax.fori_loop(0, NY, toeplitz, jnp.zeros((128, 128), f32))

    arrived(col_all(yr), y_sem)
    for k in range(8):
        for p in range(8 - k):
            for par in range(2):
                at = k * 256 + par * 128
                lhs[16 * (p + k) : 16 * (p + k + 1), at : at + 128] = yr[p, par]

    @pl.loop(0, 8)
    def _(i):
        right = []
        for k in range(8):
            r0 = pl.multiple_of(14464 - 2048 * k + 256 * i, 128)
            r1 = pl.multiple_of(14336 - 2048 * k + 256 * i, 128)
            right.append(jnp.concatenate([toep[pl.ds(r0, 256), :], toep[pl.ds(r1, 256), :]], axis=1))
        acc[8:, :] = acc[6 : 6 + 128, :] + jnp.dot(
            lhs[...], jnp.concatenate(right, axis=0), preferred_element_type=f32
        )

    ys2[...] = acc[8:, :].astype(bf16).reshape(NY, 16, 256)
    col_exchange(lambda p: ys2.at[p], yr2, y2_sem)
    yr2[y] = ys2[y]
    arrived(halo_r.at[q], halo_sem, 2)
    query_t[...] = short_conv(0).T
    pltpu.make_async_copy(ob, ob, o_sem).wait()
    left(halo_s, halo_sem)
    left(row_all(fs), f_sem)
    left(row_all(xs), x_sem)
    left(col_all(hr), h_sem)
    left(col_all(ys), y_sem)
    arrived(col_all(yr2), y2_sem)
    back = jnp.dot(
        perm2[...], yr2[...].reshape(128, 256), preferred_element_type=f32
    ).astype(bf16)
    for b in range(8):
        for par in range(2):
            xs2[2 * b + par] = back[16 * b : 16 * b + 16, 128 * par : 128 * par + 128]
    def give(e, dc):
        p = rowpeer(e, dc)
        there = (8 - e) % 8
        send(xs2.at[p], xr2.at[2 * there + dc], x2_sem, y * NX + p, z, 1 + there // 2).start()

    row_loop(give)
    xr2[0] = xs2[xc]

    def zsend(g, o_block, o_to, k=None):
        at = hid.at[g, (z + o_block) % NZ]
        send(at, at, z_sem, ctx, (z + o_to) % NZ, 1 + g if k is None else k).start()

    relayed = (0, 3, 1)

    def own(g):
        arrived(xr2.at[pl.ds(1, 3) if g == 0 else pl.ds(4 * g, 4)], x2_sem, 1 + g)
        for k in range(4):
            at = pl.ds(pl.multiple_of(rowpeer(2 * g + k // 2, k % 2) * 16, 16), 16)
            hid[g, z, k] = (query_t[at, :] * (xr2[4 * g + k].astype(f32) + direct_t[at, :])).astype(bf16)
        if g not in relayed:
            zsend(g, 0, 4)
            zsend(g, 0, 5)
        else:
            zsend(g, 0, 5, 5 + g)
        for o in (3, 6, 2, 7, 1):
            zsend(g, 0, o)

    def relay(g):
        arrived(hid.at[g, (z + 3) % NZ], z_sem, 5 + g)
        zsend(g, 3, 7)

    def out_part(g):
        arrived(hid.at[g, pl.ds(0, 6 if g in relayed else 7)], z_sem, 1 + g)
        return lax.dot_general(
            hid[g].reshape(NZ * 64, ROWS), ob[g].reshape(NZ * 64, FEATS),
            (((0,), (0,)), ((), ())), preferred_element_type=f32)

    own(0)
    own(3)
    own(1)
    relay(0)
    own(2)
    relay(3)
    relay(1)
    oacc[...] = out_part(0)
    oacc[...] += out_part(3)
    oacc[...] += out_part(1)
    left(col_all(ys2), y2_sem)
    left(row_all(xs2), x2_sem)
    out_ref[...] = (oacc[...] + out_part(2)).astype(bf16)
    for g in range(4):
        left(hid.at[g, pl.ds(0, 7)], z_sem)


def per_device(hidden_in, in_proj, short_taps, long_filters, skip_gain, out_proj):
    f32, bf16 = jnp.float32, jnp.bfloat16
    VMEM, DMA = pltpu.VMEM, pltpu.SemaphoreType.DMA
    scratch = [
        VMEM((ROWS, MODEL), bf16),
        VMEM((3, MODEL, CHAN), bf16),
        VMEM((4, NZ, 4, 16, FEATS), bf16),
        VMEM((3, 3, CHAN), bf16),
        VMEM((NX, ROWS), f32),
        VMEM((1, CHAN), f32),
        VMEM((3, ROWS, CHAN), f32),
        VMEM((3, 8, CHAN), bf16),
        VMEM((3, 8, CHAN), bf16),
        VMEM((3, ROWS + 8, CHAN), f32),
        VMEM((CHAN, ROWS), f32),
        VMEM((CHAN, ROWS), f32),
        VMEM((NX, 1, ROWS), f32),
        VMEM((NX, 1, ROWS), f32),
        VMEM((NX, ROWS), f32),
        VMEM((NY, NX, ROWS), f32),
        VMEM((TOEP, 128), bf16),
        VMEM((256, 256), bf16),
        VMEM((128, 128), bf16),
        VMEM((128, 2048), bf16),
        VMEM((NX, 16, ROWS), bf16),
        VMEM((NX, 16, ROWS), bf16),
        VMEM((NY, 2, 16, ROWS), bf16),
        VMEM((NY, 2, 16, ROWS), bf16),
        VMEM((136, 256), f32),
        VMEM((NY, 16, 256), bf16),
        VMEM((NY, 16, 256), bf16),
        VMEM((NX, 16, ROWS), bf16),
        VMEM((NX, 16, ROWS), bf16),
        VMEM((4, NZ, 4, 16, ROWS), bf16),
        VMEM((ROWS, FEATS), f32),
        DMA((4,)),
        DMA((3, NK)),
        DMA,
        DMA((3,)),
        DMA((2,)),
        DMA((2,)),
        DMA((2,)),
        DMA((2,)),
        DMA((2,)),
        DMA((5,)),
        DMA((9,)),
    ]
    return pl.pallas_call(
        kernel,
        out_shape=jax.ShapeDtypeStruct((ROWS, FEATS), bf16),
        in_specs=[pl.BlockSpec(memory_space=pl.ANY)] * 6,
        out_specs=pl.BlockSpec(memory_space=pltpu.VMEM),
        scratch_shapes=scratch,
        compiler_params=pltpu.CompilerParams(
            collective_id=0, has_side_effects=True, vmem_limit_bytes=67043328
        ),
    )(
        hidden_in,
        jnp.transpose(in_proj, (1, 0, 2)),
        short_taps,
        long_filters.T,
        skip_gain.reshape(1, CHAN),
        out_proj.reshape(NZ, NX, 16, FEATS),
    )


def solution(mesh):
    in_specs = (
        P("ctx", None),
        P(None, None, "tp"),
        P(None, None, "tp"),
        P("ctx", "tp"),
        P("tp"),
        P(None, "tp"),
    )
    return jax.shard_map(
        per_device, mesh=mesh, in_specs=in_specs, out_specs=P("ctx", "tp"), check_vma=False
    )
```

```python
import functools

import jax
import jax.numpy as jnp
from jax import lax
from jax.experimental import pallas as pl
from jax.experimental.pallas import tpu as pltpu
from jax.sharding import PartitionSpec as P

MESH = pl.DeviceIdType.MESH
NX = 16
NY = 8
NZ = 8
ROWS = 128
CHAN = 256
MODEL = 4096
FEATS = 512
KCH = 1024
NK = MODEL // KCH
TOEP = 16512


def kernel(
    x_hbm, w_hbm, taps_hbm, filt_hbm, skip_hbm, o_hbm, out_ref,
    xb, wb, ob, taps_v, filt_v, skip_v,
    pacc, halo_s, halo_r, ext, query_t, direct_t,
    fs, fr, hs, hr, toep, perm1, perm2, lhs,
    xs, xr, ys, yr, acc, ys2, yr2, xs2, xr2, hid, oacc,
    in_sem, w_sem, o_sem, halo_sem, f_sem, h_sem, x_sem, y_sem, y2_sem, x2_sem, z_sem,
):
    f32, bf16 = jnp.float32, jnp.bfloat16
    ctx = lax.axis_index("ctx")
    z = lax.axis_index("tp")
    y, xc = ctx // NX, ctx % NX
    x, core = xc // 2, xc % 2
    nxt, prv = (ctx + 1) % (NX * NY), (ctx + NX * NY - 1) % (NX * NY)

    def chip(t):
        return 4 + (t + 1) // 2 * (1 - 2 * (t % 2))

    def rowpeer(e, dc):
        return (x + e) % 8 * 2 + (core + dc) % 2

    def row_loop(one):
        @pl.loop(0, 7)
        def _(t):
            one(chip(t), 0)
            one(chip(t), 1)

        one(0, 1)

    copies = [
        pltpu.make_async_copy(x_hbm, xb, in_sem.at[0]),
        pltpu.make_async_copy(taps_hbm, taps_v, in_sem.at[1]),
        pltpu.make_async_copy(filt_hbm, filt_v, in_sem.at[2]),
        pltpu.make_async_copy(skip_hbm, skip_v, in_sem.at[3]),
    ]

    def wcopy(j, c):
        at = pl.ds(c * KCH, KCH)
        return pltpu.make_async_copy(w_hbm.at[j, at], wb.at[j, at], w_sem.at[j, c])

    def ocopy(k):
        p = rowpeer(k // 2, k % 2)
        return pltpu.make_async_copy(o_hbm.at[:, p], ob.at[k // 4, :, k % 4], o_sem)

    copies[2].start()
    copies[0].start()
    for j in (1, 2):
        for c in range(NK):
            wcopy(j, c).start()
    copies[1].start()
    copies[3].start()

    barrier = pltpu.get_barrier_semaphore()

    def greet(c, t):
        pl.semaphore_signal(barrier, inc=1, device_id=(c, t), device_id_type=MESH)

    row_loop(lambda e, dc: greet(y * NX + rowpeer(e, dc), z))

    @pl.loop(1, 8)
    def _(o):
        greet((y + o) % NY * NX + xc, z)
        greet(ctx, (z + o) % NZ)

    greet(nxt, z)
    greet(prv, z)

    row = lax.broadcasted_iota(jnp.int32, (256, 256), 0)
    col = lax.broadcasted_iota(jnp.int32, (256, 256), 1)
    take = (row % 16 // 2 * 2 + row // 16 % 2) * 16 + row // 32 * 2 + row % 2
    perm1[...] = jnp.where(col == take, 1.0, 0.0).astype(bf16)
    row = lax.broadcasted_iota(jnp.int32, (128, 128), 0)
    col = lax.broadcasted_iota(jnp.int32, (128, 128), 1)
    perm2[...] = jnp.where(col == (row % 16 // 2) * 16 + row // 16 * 2 + row % 2, 1.0, 0.0).astype(bf16)
    pacc[...] = jnp.zeros_like(pacc)
    acc[...] = jnp.zeros_like(acc)
    for k in range(1, 8):
        lhs[: 16 * k, k * 256 : (k + 1) * 256] = jnp.zeros((16 * k, 256), bf16)
    toep[128 * 128 :, :] = jnp.zeros((128, 128), bf16)

    def send(src, dst, sems, c, t, k=1):
        return pltpu.make_async_remote_copy(
            src_ref=src, dst_ref=dst, send_sem=sems.at[0], recv_sem=sems.at[k],
            device_id=(c, t), device_id_type=MESH)

    def arrived(at, sems, k=1):
        send(at, at, sems, ctx, z, k).wait_recv()

    def left(at, sems):
        send(at, at, sems, ctx, z).wait_send()

    def row_exchange(src, dst, sems):
        def one(e, dc):
            p = rowpeer(e, dc)
            send(src.at[p], dst.at[xc], sems, y * NX + p, z).start()

        row_loop(one)

    def row_all(at):
        return at.at[pl.ds(0, NX - 1)]

    def col_exchange(src_of, dst, sems):
        @pl.loop(0, 7)
        def _(t):
            p = (y + chip(t)) % NY
            send(src_of(p), dst.at[y], sems, p * NX + xc, z).start()

    def col_all(at):
        return at.at[pl.ds(0, NY - 1)]

    copies[2].wait()
    for f in range(NX):
        fs[f] = filt_v[f : f + 1, :]
    pl.semaphore_wait(barrier, NX - 1 + NY - 1 + 2 + NZ - 1)
    row_exchange(fs, fr, f_sem)
    fr[xc] = fs[xc]

    copies[0].wait()

    def project(j, c):
        wcopy(j, c).wait()
        at = pl.ds(pl.multiple_of(c * KCH, KCH), KCH)
        pacc[j] += jnp.dot(xb[:, at], wb[j, at, :], preferred_element_type=f32)

    def projected(j):
        rounded = pacc[j].astype(bf16)
        ext[j, 8:, :] = rounded.astype(f32)
        halo_s[j] = rounded[ROWS - 8 :, :]

    kv, q = pl.ds(1, 2), pl.ds(0, 1)

    def short_conv(j):
        before = halo_r[j].astype(f32)
        ext[j, :8, :] = jnp.where(ctx == 0, jnp.zeros_like(before), before)
        taps = [taps_v[i].astype(f32)[j : j + 1, :] for i in range(3)]
        return (
            taps[0] * ext[j, 8:, :]
            + taps[1] * ext[j, 7 : 7 + ROWS, :]
            + taps[2] * ext[j, 6 : 6 + ROWS, :]
        )


    @pl.loop(0, 2 * NK)
    def _(i):
        project(1 + i // NK, i % NK)

    projected(1)
    projected(2)
    for c in range(NK):
        wcopy(0, c).start()
    send(halo_s.at[kv], halo_r.at[kv], halo_sem, nxt, z).start()

    copies[1].wait()
    copies[3].wait()
    arrived(halo_r.at[kv], halo_sem)
    keyed = short_conv(1)
    gated = keyed * short_conv(2)
    xs[...] = gated.T.astype(bf16).reshape(NX, 16, ROWS)
    row_exchange(xs, xr, x_sem)
    xr[xc] = xs[xc]

    arrived(row_all(fr), f_sem)
    hs[...] = fr[...].reshape(NX, ROWS)
    col_exchange(lambda p: hs, hr, h_sem)
    hr[y] = hs[...]

    @pl.loop(0, NK)
    def _(c):
        project(0, c)

    projected(0)
    send(halo_s.at[q], halo_r.at[q], halo_sem, nxt, z, 2).start()
    direct_t[...] = (skip_v[...] * gated).T

    arrived(row_all(xr), x_sem)
    ys[...] = jnp.dot(
        perm1[...], xr[...].reshape(256, ROWS), preferred_element_type=f32
    ).astype(bf16).reshape(NY, 2, 16, ROWS)
    col_exchange(lambda p: ys.at[p], yr, y_sem)
    yr[y] = ys[y]

    @pl.loop(0, NX)
    def _(k):
        ocopy(k).start()


    lane = lax.broadcasted_iota(jnp.int32, (128, 128), 1)
    sub = lax.broadcasted_iota(jnp.int32, (128, 128), 0)
    keep = lane >= sub

    arrived(col_all(hr), h_sem)

    def toeplitz(p, before):
        for j in range(16):
            line = hr[p, j : j + 1, :]
            now = pltpu.roll(jnp.broadcast_to(line, (128, 128)), 0, 1, stride=1, stride_axis=0)
            at = pl.multiple_of((127 - j) * 128 - p * 2048, 128)
            toep[pl.ds(at, 128), :] = jnp.where(keep, now, before).astype(bf16)
            before = now
        return before

    lax.fori_loop(0, NY, toeplitz, jnp.zeros((128, 128), f32))

    arrived(col_all(yr), y_sem)
    for k in range(8):
        for p in range(8 - k):
            for par in range(2):
                at = k * 256 + par * 128
                lhs[16 * (p + k) : 16 * (p + k + 1), at : at + 128] = yr[p, par]

    @pl.loop(0, 8)
    def _(i):
        right = []
        for k in range(8):
            r0 = pl.multiple_of(14464 - 2048 * k + 256 * i, 128)
            r1 = pl.multiple_of(14336 - 2048 * k + 256 * i, 128)
            right.append(jnp.concatenate([toep[pl.ds(r0, 256), :], toep[pl.ds(r1, 256), :]], axis=1))
        acc[8:, :] = acc[6 : 6 + 128, :] + jnp.dot(
            lhs[...], jnp.concatenate(right, axis=0), preferred_element_type=f32
        )

    ys2[...] = acc[8:, :].astype(bf16).reshape(NY, 16, 256)
    col_exchange(lambda p: ys2.at[p], yr2, y2_sem)
    yr2[y] = ys2[y]
    arrived(halo_r.at[q], halo_sem, 2)
    query_t[...] = short_conv(0).T
    pltpu.make_async_copy(ob, ob, o_sem).wait()
    left(halo_s, halo_sem)
    left(row_all(fs), f_sem)
    left(row_all(xs), x_sem)
    left(col_all(hr), h_sem)
    left(col_all(ys), y_sem)
    arrived(col_all(yr2), y2_sem)
    back = jnp.dot(
        perm2[...], yr2[...].reshape(128, 256), preferred_element_type=f32
    ).astype(bf16)
    for b in range(8):
        for par in range(2):
            xs2[2 * b + par] = back[16 * b : 16 * b + 16, 128 * par : 128 * par + 128]
    def give(e, dc):
        p = rowpeer(e, dc)
        there = (8 - e) % 8
        send(xs2.at[p], xr2.at[2 * there + dc], x2_sem, y * NX + p, z, 1 + there // 2).start()

    row_loop(give)
    xr2[0] = xs2[xc]

    def zsend(g, o_block, o_to, k=None):
        at = hid.at[g, (z + o_block) % NZ]
        send(at, at, z_sem, ctx, (z + o_to) % NZ, 1 + g if k is None else k).start()

    relayed = (0, 3, 1)

    def own(g):
        arrived(xr2.at[pl.ds(1, 3) if g == 0 else pl.ds(4 * g, 4)], x2_sem, 1 + g)
        for k in range(4):
            at = pl.ds(pl.multiple_of(rowpeer(2 * g + k // 2, k % 2) * 16, 16), 16)
            hid[g, z, k] = (query_t[at, :] * (xr2[4 * g + k].astype(f32) + direct_t[at, :])).astype(bf16)
        if g not in relayed:
            zsend(g, 0, 4)
            zsend(g, 0, 5)
        else:
            zsend(g, 0, 5, 5 + g)
        for o in (3, 6, 2, 7, 1):
            zsend(g, 0, o)

    def relay(g):
        arrived(hid.at[g, (z + 3) % NZ], z_sem, 5 + g)
        zsend(g, 3, 7)

    def out_part(g):
        arrived(hid.at[g, pl.ds(0, 6 if g in relayed else 7)], z_sem, 1 + g)
        return lax.dot_general(
            hid[g].reshape(NZ * 64, ROWS), ob[g].reshape(NZ * 64, FEATS),
            (((0,), (0,)), ((), ())), preferred_element_type=f32)

    own(0)
    own(3)
    own(1)
    relay(0)
    own(2)
    relay(3)
    relay(1)
    oacc[...] = out_part(0)
    oacc[...] += out_part(3)
    oacc[...] += out_part(1)
    left(col_all(ys2), y2_sem)
    left(row_all(xs2), x2_sem)
    out_ref[...] = (oacc[...] + out_part(2)).astype(bf16)
    for g in range(4):
        left(hid.at[g, pl.ds(0, 7)], z_sem)


def per_device(hidden_in, in_proj, short_taps, long_filters, skip_gain, out_proj):
    f32, bf16 = jnp.float32, jnp.bfloat16
    VMEM, DMA = pltpu.VMEM, pltpu.SemaphoreType.DMA
    scratch = [
        VMEM((ROWS, MODEL), bf16),
        VMEM((3, MODEL, CHAN), bf16),
        VMEM((4, NZ, 4, 16, FEATS), bf16),
        VMEM((3, 3, CHAN), bf16),
        VMEM((NX, ROWS), f32),
        VMEM((1, CHAN), f32),
        VMEM((3, ROWS, CHAN), f32),
        VMEM((3, 8, CHAN), bf16),
        VMEM((3, 8, CHAN), bf16),
        VMEM((3, ROWS + 8, CHAN), f32),
        VMEM((CHAN, ROWS), f32),
        VMEM((CHAN, ROWS), f32),
        VMEM((NX, 1, ROWS), f32),
        VMEM((NX, 1, ROWS), f32),
        VMEM((NX, ROWS), f32),
        VMEM((NY, NX, ROWS), f32),
        VMEM((TOEP, 128), bf16),
        VMEM((256, 256), bf16),
        VMEM((128, 128), bf16),
        VMEM((128, 2048), bf16),
        VMEM((NX, 16, ROWS), bf16),
        VMEM((NX, 16, ROWS), bf16),
        VMEM((NY, 2, 16, ROWS), bf16),
        VMEM((NY, 2, 16, ROWS), bf16),
        VMEM((136, 256), f32),
        VMEM((NY, 16, 256), bf16),
        VMEM((NY, 16, 256), bf16),
        VMEM((NX, 16, ROWS), bf16),
        VMEM((NX, 16, ROWS), bf16),
        VMEM((4, NZ, 4, 16, ROWS), bf16),
        VMEM((ROWS, FEATS), f32),
        DMA((4,)),
        DMA((3, NK)),
        DMA,
        DMA((3,)),
        DMA((2,)),
        DMA((2,)),
        DMA((2,)),
        DMA((2,)),
        DMA((2,)),
        DMA((5,)),
        DMA((9,)),
    ]
    return pl.pallas_call(
        kernel,
        out_shape=jax.ShapeDtypeStruct((ROWS, FEATS), bf16),
        in_specs=[pl.BlockSpec(memory_space=pl.ANY)] * 6,
        out_specs=pl.BlockSpec(memory_space=pltpu.VMEM),
        scratch_shapes=scratch,
        compiler_params=pltpu.CompilerParams(
            collective_id=0, has_side_effects=True, vmem_limit_bytes=67043328
        ),
    )(
        hidden_in,
        jnp.transpose(in_proj, (1, 0, 2)),
        short_taps,
        long_filters.T,
        skip_gain.reshape(1, CHAN),
        out_proj.reshape(NZ, NX, 16, FEATS),
    )


def solution(mesh):
    in_specs = (
        P("ctx", None),
        P(None, None, "tp"),
        P(None, None, "tp"),
        P("ctx", "tp"),
        P("tp"),
        P(None, "tp"),
    )
    return jax.shard_map(
        per_device, mesh=mesh, in_specs=in_specs, out_specs=P("ctx", "tp"), check_vma=False
    )
```

```python
import functools

import jax
import jax.numpy as jnp
from jax import lax
from jax.experimental import pallas as pl
from jax.experimental.pallas import tpu as pltpu
from jax.sharding import PartitionSpec as P

MESH = pl.DeviceIdType.MESH
NX = 16
NY = 8
NZ = 8
ROWS = 128
CHAN = 256
MODEL = 4096
FEATS = 512
KCH = 1024
NK = MODEL // KCH
TOEP = 16512


def kernel(
    x_hbm, w_hbm, taps_hbm, filt_hbm, skip_hbm, o_hbm, out_ref,
    xb, wb, ob, taps_v, filt_v, skip_v,
    pacc, halo_s, halo_r, ext, query_t, direct_t,
    fs, fr, hs, hr, toep, perm1, perm2, lhs,
    xs, xr, ys, yr, acc, ys2, yr2, xs2, xr2, hid, oacc,
    in_sem, xi_sem, w_sem, o_sem, halo_sem, f_sem, h_sem, x_sem, y_sem, y2_sem, x2_sem, z_sem,
):
    f32, bf16 = jnp.float32, jnp.bfloat16
    ctx = lax.axis_index("ctx")
    z = lax.axis_index("tp")
    y, xc = ctx // NX, ctx % NX
    x, core = xc // 2, xc % 2
    nxt, prv = (ctx + 1) % (NX * NY), (ctx + NX * NY - 1) % (NX * NY)

    def chip(t):
        return 4 + (t + 1) // 2 * (1 - 2 * (t % 2))

    def rowpeer(e, dc):
        return (x + e) % 8 * 2 + (core + dc) % 2

    def row_loop(one):
        @pl.loop(0, 7)
        def _(t):
            one(chip(t), 0)
            one(chip(t), 1)

        one(0, 1)

    copies = [
        pltpu.make_async_copy(taps_hbm, taps_v, in_sem.at[0]),
        pltpu.make_async_copy(filt_hbm, filt_v, in_sem.at[1]),
        pltpu.make_async_copy(skip_hbm, skip_v, in_sem.at[2]),
    ]

    def xcopy(c):
        at = pl.ds(c * KCH, KCH)
        return pltpu.make_async_copy(x_hbm.at[:, at], xb.at[:, at], xi_sem.at[c])

    def wcopy(j, c):
        at = pl.ds(c * KCH, KCH)
        return pltpu.make_async_copy(w_hbm.at[j, at], wb.at[j, at], w_sem.at[j, c])

    def ocopy(k):
        p = rowpeer(k // 2, k % 2)
        return pltpu.make_async_copy(o_hbm.at[:, p], ob.at[k // 4, :, k % 4], o_sem)

    for c in range(NK):
        xcopy(c).start()
        wcopy(1, c).start()
        wcopy(2, c).start()
    for copy in copies:
        copy.start()

    barrier = pltpu.get_barrier_semaphore()

    def greet(c, t):
        pl.semaphore_signal(barrier, inc=1, device_id=(c, t), device_id_type=MESH)

    row_loop(lambda e, dc: greet(y * NX + rowpeer(e, dc), z))

    @pl.loop(1, 8)
    def _(o):
        greet((y + o) % NY * NX + xc, z)
        greet(ctx, (z + o) % NZ)

    greet(nxt, z)
    greet(prv, z)

    row = lax.broadcasted_iota(jnp.int32, (256, 256), 0)
    col = lax.broadcasted_iota(jnp.int32, (256, 256), 1)
    take = (row % 16 // 2 * 2 + row // 16 % 2) * 16 + row // 32 * 2 + row % 2
    perm1[...] = jnp.where(col == take, 1.0, 0.0).astype(bf16)
    row = lax.broadcasted_iota(jnp.int32, (128, 128), 0)
    col = lax.broadcasted_iota(jnp.int32, (128, 128), 1)
    perm2[...] = jnp.where(col == (row % 16 // 2) * 16 + row // 16 * 2 + row % 2, 1.0, 0.0).astype(bf16)
    pacc[...] = jnp.zeros_like(pacc)
    acc[...] = jnp.zeros_like(acc)
    for k in range(1, 8):
        lhs[: 16 * k, k * 256 : (k + 1) * 256] = jnp.zeros((16 * k, 256), bf16)
    toep[128 * 128 :, :] = jnp.zeros((128, 128), bf16)

    def send(src, dst, sems, c, t, k=1):
        return pltpu.make_async_remote_copy(
            src_ref=src, dst_ref=dst, send_sem=sems.at[0], recv_sem=sems.at[k],
            device_id=(c, t), device_id_type=MESH)

    def arrived(at, sems, k=1):
        send(at, at, sems, ctx, z, k).wait_recv()

    def left(at, sems):
        send(at, at, sems, ctx, z).wait_send()

    def row_exchange(src, dst, sems):
        def one(e, dc):
            p = rowpeer(e, dc)
            send(src.at[p], dst.at[xc], sems, y * NX + p, z).start()

        row_loop(one)

    def row_all(at):
        return at.at[pl.ds(0, NX - 1)]

    def col_exchange(src_of, dst, sems):
        @pl.loop(0, 7)
        def _(t):
            p = (y + chip(t)) % NY
            send(src_of(p), dst.at[y], sems, p * NX + xc, z).start()

    def col_all(at):
        return at.at[pl.ds(0, NY - 1)]


    def projected(j):
        rounded = pacc[j].astype(bf16)
        ext[j, 8:, :] = rounded.astype(f32)
        halo_s[j] = rounded[ROWS - 8 :, :]

    kv, q = pl.ds(1, 2), pl.ds(0, 1)

    def short_conv(j):
        before = halo_r[j].astype(f32)
        ext[j, :8, :] = jnp.where(ctx == 0, jnp.zeros_like(before), before)
        taps = [taps_v[i].astype(f32)[j : j + 1, :] for i in range(3)]
        return (
            taps[0] * ext[j, 8:, :]
            + taps[1] * ext[j, 7 : 7 + ROWS, :]
            + taps[2] * ext[j, 6 : 6 + ROWS, :]
        )

    copies[1].wait()
    for f in range(NX):
        fs[f] = filt_v[f : f + 1, :]

    @pl.loop(0, NK)
    def _(c):
        for copy in (xcopy(c), wcopy(1, c), wcopy(2, c)):
            copy.wait()
        at = pl.ds(pl.multiple_of(c * KCH, KCH), KCH)
        both = jnp.dot(
            xb[:, at], jnp.concatenate([wb[1, at, :], wb[2, at, :]], axis=1), preferred_element_type=f32
        )
        pacc[1] += both[:, :CHAN]
        pacc[2] += both[:, CHAN:]

    projected(1)
    projected(2)
    for c in range(NK):
        wcopy(0, c).start()
    pl.semaphore_wait(barrier, NX - 1 + NY - 1 + 2 + NZ - 1)
    send(halo_s.at[kv], halo_r.at[kv], halo_sem, nxt, z).start()

    row_exchange(fs, fr, f_sem)
    fr[xc] = fs[xc]
    copies[0].wait()
    copies[2].wait()
    arrived(halo_r.at[kv], halo_sem)
    keyed = short_conv(1)
    gated = keyed * short_conv(2)
    xs[...] = gated.T.astype(bf16).reshape(NX, 16, ROWS)
    row_exchange(xs, xr, x_sem)
    xr[xc] = xs[xc]

    arrived(row_all(fr), f_sem)
    hs[...] = fr[...].reshape(NX, ROWS)
    col_exchange(lambda p: hs, hr, h_sem)
    hr[y] = hs[...]

    @pl.loop(0, NK)
    def _(c):
        wcopy(0, c).wait()
        at = pl.ds(pl.multiple_of(c * KCH, KCH), KCH)
        pacc[0] += jnp.dot(xb[:, at], wb[0, at, :], preferred_element_type=f32)

    projected(0)
    send(halo_s.at[q], halo_r.at[q], halo_sem, nxt, z, 2).start()
    direct_t[...] = (skip_v[...] * gated).T

    arrived(row_all(xr), x_sem)
    ys[...] = jnp.dot(
        perm1[...], xr[...].reshape(256, ROWS), preferred_element_type=f32
    ).astype(bf16).reshape(NY, 2, 16, ROWS)
    col_exchange(lambda p: ys.at[p], yr, y_sem)
    yr[y] = ys[y]

    @pl.loop(0, NX)
    def _(k):
        ocopy(k).start()


    lane = lax.broadcasted_iota(jnp.int32, (128, 128), 1)
    sub = lax.broadcasted_iota(jnp.int32, (128, 128), 0)
    keep = lane >= sub

    arrived(col_all(hr), h_sem)

    def toeplitz(p, before):
        for j in range(16):
            line = hr[p, j : j + 1, :]
            now = pltpu.roll(jnp.broadcast_to(line, (128, 128)), 0, 1, stride=1, stride_axis=0)
            at = pl.multiple_of((127 - j) * 128 - p * 2048, 128)
            toep[pl.ds(at, 128), :] = jnp.where(keep, now, before).astype(bf16)
            before = now
        return before

    lax.fori_loop(0, NY, toeplitz, jnp.zeros((128, 128), f32))

    arrived(col_all(yr), y_sem)
    for k in range(8):
        for p in range(8 - k):
            for par in range(2):
                at = k * 256 + par * 128
                lhs[16 * (p + k) : 16 * (p + k + 1), at : at + 128] = yr[p, par]

    @pl.loop(0, 8)
    def _(i):
        right = []
        for k in range(8):
            r0 = pl.multiple_of(14464 - 2048 * k + 256 * i, 128)
            r1 = pl.multiple_of(14336 - 2048 * k + 256 * i, 128)
            right.append(jnp.concatenate([toep[pl.ds(r0, 256), :], toep[pl.ds(r1, 256), :]], axis=1))
        acc[8:, :] = acc[6 : 6 + 128, :] + jnp.dot(
            lhs[...], jnp.concatenate(right, axis=0), preferred_element_type=f32
        )

    ys2[...] = acc[8:, :].astype(bf16).reshape(NY, 16, 256)
    col_exchange(lambda p: ys2.at[p], yr2, y2_sem)
    yr2[y] = ys2[y]
    arrived(halo_r.at[q], halo_sem, 2)
    query_t[...] = short_conv(0).T
    pltpu.make_async_copy(ob, ob, o_sem).wait()
    left(halo_s, halo_sem)
    left(row_all(fs), f_sem)
    left(row_all(xs), x_sem)
    left(col_all(hr), h_sem)
    left(col_all(ys), y_sem)
    arrived(col_all(yr2), y2_sem)
    back = jnp.dot(
        perm2[...], yr2[...].reshape(128, 256), preferred_element_type=f32
    ).astype(bf16)
    for b in range(8):
        for par in range(2):
            xs2[2 * b + par] = back[16 * b : 16 * b + 16, 128 * par : 128 * par + 128]
    def give(e, dc):
        p = rowpeer(e, dc)
        there = (8 - e) % 8
        send(xs2.at[p], xr2.at[2 * there + dc], x2_sem, y * NX + p, z, 1 + there // 2).start()

    row_loop(give)
    xr2[0] = xs2[xc]

    def zsend(g, o_block, o_to, k=None):
        at = hid.at[g, (z + o_block) % NZ]
        send(at, at, z_sem, ctx, (z + o_to) % NZ, 1 + g if k is None else k).start()

    relayed = (0, 3, 1)

    def own(g):
        arrived(xr2.at[pl.ds(1, 3) if g == 0 else pl.ds(4 * g, 4)], x2_sem, 1 + g)
        for k in range(4):
            at = pl.ds(pl.multiple_of(rowpeer(2 * g + k // 2, k % 2) * 16, 16), 16)
            hid[g, z, k] = (query_t[at, :] * (xr2[4 * g + k].astype(f32) + direct_t[at, :])).astype(bf16)
        if g not in relayed:
            zsend(g, 0, 4)
            zsend(g, 0, 5)
        else:
            zsend(g, 0, 5, 5 + g)
        for o in (3, 6, 2, 7, 1):
            zsend(g, 0, o)

    def relay(g):
        arrived(hid.at[g, (z + 3) % NZ], z_sem, 5 + g)
        zsend(g, 3, 7)

    def out_part(g):
        arrived(hid.at[g, pl.ds(0, 6 if g in relayed else 7)], z_sem, 1 + g)
        return lax.dot_general(
            hid[g].reshape(NZ * 64, ROWS), ob[g].reshape(NZ * 64, FEATS),
            (((0,), (0,)), ((), ())), preferred_element_type=f32)

    own(0)
    own(3)
    own(1)
    relay(0)
    own(2)
    relay(3)
    relay(1)
    oacc[...] = out_part(0)
    oacc[...] += out_part(3)
    oacc[...] += out_part(1)
    left(col_all(ys2), y2_sem)
    left(row_all(xs2), x2_sem)
    out_ref[...] = (oacc[...] + out_part(2)).astype(bf16)
    for g in range(4):
        left(hid.at[g, pl.ds(0, 7)], z_sem)


def per_device(hidden_in, in_proj, short_taps, long_filters, skip_gain, out_proj):
    f32, bf16 = jnp.float32, jnp.bfloat16
    VMEM, DMA = pltpu.VMEM, pltpu.SemaphoreType.DMA
    scratch = [
        VMEM((ROWS, MODEL), bf16),
        VMEM((3, MODEL, CHAN), bf16),
        VMEM((4, NZ, 4, 16, FEATS), bf16),
        VMEM((3, 3, CHAN), bf16),
        VMEM((NX, ROWS), f32),
        VMEM((1, CHAN), f32),
        VMEM((3, ROWS, CHAN), f32),
        VMEM((3, 8, CHAN), bf16),
        VMEM((3, 8, CHAN), bf16),
        VMEM((3, ROWS + 8, CHAN), f32),
        VMEM((CHAN, ROWS), f32),
        VMEM((CHAN, ROWS), f32),
        VMEM((NX, 1, ROWS), f32),
        VMEM((NX, 1, ROWS), f32),
        VMEM((NX, ROWS), f32),
        VMEM((NY, NX, ROWS), f32),
        VMEM((TOEP, 128), bf16),
        VMEM((256, 256), bf16),
        VMEM((128, 128), bf16),
        VMEM((128, 2048), bf16),
        VMEM((NX, 16, ROWS), bf16),
        VMEM((NX, 16, ROWS), bf16),
        VMEM((NY, 2, 16, ROWS), bf16),
        VMEM((NY, 2, 16, ROWS), bf16),
        VMEM((136, 256), f32),
        VMEM((NY, 16, 256), bf16),
        VMEM((NY, 16, 256), bf16),
        VMEM((NX, 16, ROWS), bf16),
        VMEM((NX, 16, ROWS), bf16),
        VMEM((4, NZ, 4, 16, ROWS), bf16),
        VMEM((ROWS, FEATS), f32),
        DMA((3,)),
        DMA((NK,)),
        DMA((3, NK)),
        DMA,
        DMA((3,)),
        DMA((2,)),
        DMA((2,)),
        DMA((2,)),
        DMA((2,)),
        DMA((2,)),
        DMA((5,)),
        DMA((9,)),
    ]
    return pl.pallas_call(
        kernel,
        out_shape=jax.ShapeDtypeStruct((ROWS, FEATS), bf16),
        in_specs=[pl.BlockSpec(memory_space=pl.ANY)] * 6,
        out_specs=pl.BlockSpec(memory_space=pltpu.VMEM),
        scratch_shapes=scratch,
        compiler_params=pltpu.CompilerParams(
            collective_id=0, has_side_effects=True, vmem_limit_bytes=67043328
        ),
    )(
        hidden_in,
        jnp.transpose(in_proj, (1, 0, 2)),
        short_taps,
        long_filters.T,
        skip_gain.reshape(1, CHAN),
        out_proj.reshape(NZ, NX, 16, FEATS),
    )


def solution(mesh):
    in_specs = (
        P("ctx", None),
        P(None, None, "tp"),
        P(None, None, "tp"),
        P("ctx", "tp"),
        P("tp"),
        P(None, "tp"),
    )
    return jax.shard_map(
        per_device, mesh=mesh, in_specs=in_specs, out_specs=P("ctx", "tp"), check_vma=False
    )
```

```python
import functools

import jax
import jax.numpy as jnp
from jax import lax
from jax.experimental import pallas as pl
from jax.experimental.pallas import tpu as pltpu
from jax.sharding import PartitionSpec as P

MESH = pl.DeviceIdType.MESH
NX = 16
NY = 8
NZ = 8
ROWS = 128
CHAN = 256
MODEL = 4096
FEATS = 512
KCH = 1024
NK = MODEL // KCH
TOEP = 16512


def kernel(
    x_hbm, w_hbm, taps_hbm, filt_hbm, skip_hbm, o_hbm, out_ref,
    xb, wb, ob, taps_v, filt_v, skip_v,
    pacc, halo_s, halo_r, ext, query_t, direct_t,
    fs, fr, hs, hr, toep, perm1, perm2, lhs,
    xs, xr, ys, yr, acc, ys2, yr2, xs2, xr2, hid, oacc,
    in_sem, xi_sem, w_sem, o_sem, halo_sem, f_sem, h_sem, x_sem, y_sem, y2_sem, x2_sem, z_sem,
):
    f32, bf16 = jnp.float32, jnp.bfloat16
    ctx = lax.axis_index("ctx")
    z = lax.axis_index("tp")
    y, xc = ctx // NX, ctx % NX
    x, core = xc // 2, xc % 2
    nxt, prv = (ctx + 1) % (NX * NY), (ctx + NX * NY - 1) % (NX * NY)

    def chip(t):
        return 4 + (t + 1) // 2 * (1 - 2 * (t % 2))

    def rowpeer(e, dc):
        return (x + e) % 8 * 2 + (core + dc) % 2

    def row_loop(one):
        @pl.loop(0, 7)
        def _(t):
            one(chip(t), 0)
            one(chip(t), 1)

        one(0, 1)

    copies = [
        pltpu.make_async_copy(taps_hbm, taps_v, in_sem.at[0]),
        pltpu.make_async_copy(filt_hbm, filt_v, in_sem.at[1]),
        pltpu.make_async_copy(skip_hbm, skip_v, in_sem.at[2]),
    ]

    def xcopy(c):
        at = pl.ds(c * KCH, KCH)
        return pltpu.make_async_copy(x_hbm.at[:, at], xb.at[:, at], xi_sem.at[c])

    def wcopy(j, c):
        at = pl.ds(c * KCH, KCH)
        return pltpu.make_async_copy(w_hbm.at[j, at], wb.at[j, at], w_sem.at[j, c])

    def ocopy(k):
        p = rowpeer(k // 2, k % 2)
        return pltpu.make_async_copy(o_hbm.at[:, p], ob.at[k // 4, :, k % 4], o_sem)

    for c in range(NK):
        xcopy(c).start()
        wcopy(1, c).start()
        wcopy(2, c).start()
    for copy in copies:
        copy.start()

    barrier = pltpu.get_barrier_semaphore()

    def greet(c, t):
        pl.semaphore_signal(barrier, inc=1, device_id=(c, t), device_id_type=MESH)

    row_loop(lambda e, dc: greet(y * NX + rowpeer(e, dc), z))

    @pl.loop(1, 8)
    def _(o):
        greet((y + o) % NY * NX + xc, z)
        greet(ctx, (z + o) % NZ)

    greet(nxt, z)
    greet(prv, z)

    row = lax.broadcasted_iota(jnp.int32, (256, 256), 0)
    col = lax.broadcasted_iota(jnp.int32, (256, 256), 1)
    take = (row % 16 // 2 * 2 + row // 16 % 2) * 16 + row // 32 * 2 + row % 2
    perm1[...] = jnp.where(col == take, 1.0, 0.0).astype(bf16)
    row = lax.broadcasted_iota(jnp.int32, (128, 128), 0)
    col = lax.broadcasted_iota(jnp.int32, (128, 128), 1)
    perm2[...] = jnp.where(col == (row % 16 // 2) * 16 + row // 16 * 2 + row % 2, 1.0, 0.0).astype(bf16)
    pacc[...] = jnp.zeros_like(pacc)
    acc[...] = jnp.zeros_like(acc)
    for k in range(1, 8):
        lhs[: 16 * k, k * 256 : (k + 1) * 256] = jnp.zeros((16 * k, 256), bf16)
    toep[128 * 128 :, :] = jnp.zeros((128, 128), bf16)

    def send(src, dst, sems, c, t, k=1):
        return pltpu.make_async_remote_copy(
            src_ref=src, dst_ref=dst, send_sem=sems.at[0], recv_sem=sems.at[k],
            device_id=(c, t), device_id_type=MESH)

    def arrived(at, sems, k=1):
        send(at, at, sems, ctx, z, k).wait_recv()

    def left(at, sems):
        send(at, at, sems, ctx, z).wait_send()

    def row_exchange(src, dst, sems):
        def one(e, dc):
            p = rowpeer(e, dc)
            send(src.at[p], dst.at[xc], sems, y * NX + p, z).start()

        row_loop(one)

    def row_all(at):
        return at.at[pl.ds(0, NX - 1)]

    def col_exchange(src_of, dst, sems):
        @pl.loop(0, 7)
        def _(t):
            p = (y + chip(t)) % NY
            send(src_of(p), dst.at[y], sems, p * NX + xc, z).start()

    def col_all(at):
        return at.at[pl.ds(0, NY - 1)]


    def projected(j):
        rounded = pacc[j].astype(bf16)
        ext[j, 8:, :] = rounded.astype(f32)
        halo_s[j] = rounded[ROWS - 8 :, :]

    kv, q = pl.ds(1, 2), pl.ds(0, 1)

    def short_conv(j):
        before = halo_r[j].astype(f32)
        ext[j, :8, :] = jnp.where(ctx == 0, jnp.zeros_like(before), before)
        taps = [taps_v[i].astype(f32)[j : j + 1, :] for i in range(3)]
        return (
            taps[0] * ext[j, 8:, :]
            + taps[1] * ext[j, 7 : 7 + ROWS, :]
            + taps[2] * ext[j, 6 : 6 + ROWS, :]
        )

    copies[1].wait()
    for f in range(NX):
        fs[f] = filt_v[f : f + 1, :]

    @pl.loop(0, NK)
    def _(c):
        for copy in (xcopy(c), wcopy(1, c), wcopy(2, c)):
            copy.wait()
        at = pl.ds(pl.multiple_of(c * KCH, KCH), KCH)
        both = jnp.dot(
            xb[:, at], jnp.concatenate([wb[1, at, :], wb[2, at, :]], axis=1), preferred_element_type=f32
        )
        pacc[1] += both[:, :CHAN]
        pacc[2] += both[:, CHAN:]

    projected(1)
    projected(2)
    for c in range(NK):
        wcopy(0, c).start()
    pl.semaphore_wait(barrier, NX - 1 + NY - 1 + 2 + NZ - 1)
    send(halo_s.at[kv], halo_r.at[kv], halo_sem, nxt, z).start()

    row_exchange(fs, fr, f_sem)
    fr[xc] = fs[xc]
    copies[0].wait()
    copies[2].wait()
    arrived(halo_r.at[kv], halo_sem)
    keyed = short_conv(1)
    gated = keyed * short_conv(2)
    xs[...] = gated.T.astype(bf16).reshape(NX, 16, ROWS)
    row_exchange(xs, xr, x_sem)
    xr[xc] = xs[xc]

    arrived(row_all(fr), f_sem)
    hs[...] = fr[...].reshape(NX, ROWS)
    col_exchange(lambda p: hs, hr, h_sem)
    hr[y] = hs[...]

    @pl.loop(0, NK)
    def _(c):
        wcopy(0, c).wait()
        at = pl.ds(pl.multiple_of(c * KCH, KCH), KCH)
        pacc[0] += jnp.dot(xb[:, at], wb[0, at, :], preferred_element_type=f32)

    projected(0)
    send(halo_s.at[q], halo_r.at[q], halo_sem, nxt, z, 2).start()
    direct_t[...] = (skip_v[...] * gated).T

    arrived(row_all(xr), x_sem)
    ys[...] = jnp.dot(
        perm1[...], xr[...].reshape(256, ROWS), preferred_element_type=f32
    ).astype(bf16).reshape(NY, 2, 16, ROWS)
    col_exchange(lambda p: ys.at[p], yr, y_sem)
    yr[y] = ys[y]

    @pl.loop(0, NX)
    def _(k):
        ocopy(k).start()


    lane = lax.broadcasted_iota(jnp.int32, (128, 128), 1)
    sub = lax.broadcasted_iota(jnp.int32, (128, 128), 0)
    keep = lane >= sub

    arrived(col_all(hr), h_sem)

    def toeplitz(p, before):
        for j in range(16):
            line = hr[p, j : j + 1, :]
            now = pltpu.roll(jnp.broadcast_to(line, (128, 128)), 0, 1, stride=1, stride_axis=0)
            at = pl.multiple_of((127 - j) * 128 - p * 2048, 128)
            toep[pl.ds(at, 128), :] = jnp.where(keep, now, before).astype(bf16)
            before = now
        return before

    lax.fori_loop(0, NY, toeplitz, jnp.zeros((128, 128), f32))

    arrived(col_all(yr), y_sem)
    for k in range(8):
        for p in range(8 - k):
            for par in range(2):
                at = k * 256 + par * 128
                lhs[16 * (p + k) : 16 * (p + k + 1), at : at + 128] = yr[p, par]

    @pl.loop(0, 4)
    def _(i):
        right = []
        for k in range(8):
            at = [pl.multiple_of(14464 - 2048 * k + 512 * i + r, 128) for r in (0, -128, 256, 128)]
            right.append(jnp.concatenate([toep[pl.ds(r, 256), :] for r in at], axis=1))
        both = jnp.dot(lhs[...], jnp.concatenate(right, axis=0), preferred_element_type=f32)
        acc[8:, :] = acc[6 : 6 + 128, :] + both[:, :256]
        acc[8:, :] = acc[6 : 6 + 128, :] + both[:, 256:]

    ys2[...] = acc[8:, :].astype(bf16).reshape(NY, 16, 256)
    col_exchange(lambda p: ys2.at[p], yr2, y2_sem)
    yr2[y] = ys2[y]
    arrived(halo_r.at[q], halo_sem, 2)
    query_t[...] = short_conv(0).T
    pltpu.make_async_copy(ob, ob, o_sem).wait()
    left(halo_s, halo_sem)
    left(row_all(fs), f_sem)
    left(row_all(xs), x_sem)
    left(col_all(hr), h_sem)
    left(col_all(ys), y_sem)
    arrived(col_all(yr2), y2_sem)
    back = jnp.dot(
        perm2[...], yr2[...].reshape(128, 256), preferred_element_type=f32
    ).astype(bf16)
    for b in range(8):
        for par in range(2):
            xs2[2 * b + par] = back[16 * b : 16 * b + 16, 128 * par : 128 * par + 128]
    def give(e, dc):
        p = rowpeer(e, dc)
        there = (8 - e) % 8
        send(xs2.at[p], xr2.at[2 * there + dc], x2_sem, y * NX + p, z, 1 + there // 2).start()

    row_loop(give)
    xr2[0] = xs2[xc]

    def zsend(g, o_block, o_to, k=None):
        at = hid.at[g, (z + o_block) % NZ]
        send(at, at, z_sem, ctx, (z + o_to) % NZ, 1 + g if k is None else k).start()

    relayed = (0, 3, 1)

    def own(g):
        arrived(xr2.at[pl.ds(1, 3) if g == 0 else pl.ds(4 * g, 4)], x2_sem, 1 + g)
        for k in range(4):
            at = pl.ds(pl.multiple_of(rowpeer(2 * g + k // 2, k % 2) * 16, 16), 16)
            hid[g, z, k] = (query_t[at, :] * (xr2[4 * g + k].astype(f32) + direct_t[at, :])).astype(bf16)
        if g not in relayed:
            zsend(g, 0, 4)
            zsend(g, 0, 5)
        else:
            zsend(g, 0, 5, 5 + g)
        for o in (3, 6, 2, 7, 1):
            zsend(g, 0, o)

    def relay(g):
        arrived(hid.at[g, (z + 3) % NZ], z_sem, 5 + g)
        zsend(g, 3, 7)

    def out_part(g):
        arrived(hid.at[g, pl.ds(0, 6 if g in relayed else 7)], z_sem, 1 + g)
        return lax.dot_general(
            hid[g].reshape(NZ * 64, ROWS), ob[g].reshape(NZ * 64, FEATS),
            (((0,), (0,)), ((), ())), preferred_element_type=f32)

    for g in (0, 3, 1, 2):
        own(g)
    for g in relayed:
        relay(g)
    oacc[...] = out_part(0)
    oacc[...] += out_part(3)
    oacc[...] += out_part(1)
    left(col_all(ys2), y2_sem)
    left(row_all(xs2), x2_sem)
    out_ref[...] = (oacc[...] + out_part(2)).astype(bf16)
    for g in range(4):
        left(hid.at[g, pl.ds(0, 7)], z_sem)


def per_device(hidden_in, in_proj, short_taps, long_filters, skip_gain, out_proj):
    f32, bf16 = jnp.float32, jnp.bfloat16
    VMEM, DMA = pltpu.VMEM, pltpu.SemaphoreType.DMA
    scratch = [
        VMEM((ROWS, MODEL), bf16),
        VMEM((3, MODEL, CHAN), bf16),
        VMEM((4, NZ, 4, 16, FEATS), bf16),
        VMEM((3, 3, CHAN), bf16),
        VMEM((NX, ROWS), f32),
        VMEM((1, CHAN), f32),
        VMEM((3, ROWS, CHAN), f32),
        VMEM((3, 8, CHAN), bf16),
        VMEM((3, 8, CHAN), bf16),
        VMEM((3, ROWS + 8, CHAN), f32),
        VMEM((CHAN, ROWS), f32),
        VMEM((CHAN, ROWS), f32),
        VMEM((NX, 1, ROWS), f32),
        VMEM((NX, 1, ROWS), f32),
        VMEM((NX, ROWS), f32),
        VMEM((NY, NX, ROWS), f32),
        VMEM((TOEP, 128), bf16),
        VMEM((256, 256), bf16),
        VMEM((128, 128), bf16),
        VMEM((128, 2048), bf16),
        VMEM((NX, 16, ROWS), bf16),
        VMEM((NX, 16, ROWS), bf16),
        VMEM((NY, 2, 16, ROWS), bf16),
        VMEM((NY, 2, 16, ROWS), bf16),
        VMEM((136, 256), f32),
        VMEM((NY, 16, 256), bf16),
        VMEM((NY, 16, 256), bf16),
        VMEM((NX, 16, ROWS), bf16),
        VMEM((NX, 16, ROWS), bf16),
        VMEM((4, NZ, 4, 16, ROWS), bf16),
        VMEM((ROWS, FEATS), f32),
        DMA((3,)),
        DMA((NK,)),
        DMA((3, NK)),
        DMA,
        DMA((3,)),
        DMA((2,)),
        DMA((2,)),
        DMA((2,)),
        DMA((2,)),
        DMA((2,)),
        DMA((5,)),
        DMA((9,)),
    ]
    return pl.pallas_call(
        kernel,
        out_shape=jax.ShapeDtypeStruct((ROWS, FEATS), bf16),
        in_specs=[pl.BlockSpec(memory_space=pl.ANY)] * 6,
        out_specs=pl.BlockSpec(memory_space=pltpu.VMEM),
        scratch_shapes=scratch,
        compiler_params=pltpu.CompilerParams(
            collective_id=0, has_side_effects=True, vmem_limit_bytes=67043328
        ),
    )(
        hidden_in,
        jnp.transpose(in_proj, (1, 0, 2)),
        short_taps,
        long_filters.T,
        skip_gain.reshape(1, CHAN),
        out_proj.reshape(NZ, NX, 16, FEATS),
    )


def solution(mesh):
    in_specs = (
        P("ctx", None),
        P(None, None, "tp"),
        P(None, None, "tp"),
        P("ctx", "tp"),
        P("tp"),
        P(None, "tp"),
    )
    return jax.shard_map(
        per_device, mesh=mesh, in_specs=in_specs, out_specs=P("ctx", "tp"), check_vma=False
    )
```

```python
import functools

import jax
import jax.numpy as jnp
from jax import lax
from jax.experimental import pallas as pl
from jax.experimental.pallas import tpu as pltpu
from jax.sharding import PartitionSpec as P

MESH = pl.DeviceIdType.MESH
NX = 16
NY = 8
NZ = 8
ROWS = 128
CHAN = 256
MODEL = 4096
FEATS = 512
KCH = 1024
NK = MODEL // KCH
TOEP = 16512


def kernel(
    x_hbm, w_hbm, taps_hbm, filt_hbm, skip_hbm, o_hbm, out_ref,
    xb, wb, ob, taps_v, filt_v, skip_v,
    pacc, halo_s, halo_r, ext, query_t, direct_t,
    fs, fr, hs, hr, toep, perm1, perm2, lhs,
    xs, xr, ys, yr, acc, ys2, yr2, xs2, xr2, hid, oacc,
    in_sem, xi_sem, w_sem, o_sem, halo_sem, f_sem, h_sem, x_sem, y_sem, y2_sem, x2_sem, z_sem,
):
    f32, bf16 = jnp.float32, jnp.bfloat16
    ctx = lax.axis_index("ctx")
    z = lax.axis_index("tp")
    y, xc = ctx // NX, ctx % NX
    x, core = xc // 2, xc % 2
    nxt, prv = (ctx + 1) % (NX * NY), (ctx + NX * NY - 1) % (NX * NY)

    def chip(t):
        return 4 + (t + 1) // 2 * (1 - 2 * (t % 2))

    def rowpeer(e, dc):
        return (x + e) % 8 * 2 + (core + dc) % 2

    def row_loop(one):
        @pl.loop(0, 7)
        def _(t):
            one(chip(t), 0)
            one(chip(t), 1)

        one(0, 1)

    copies = [
        pltpu.make_async_copy(taps_hbm, taps_v, in_sem.at[0]),
        pltpu.make_async_copy(filt_hbm, filt_v, in_sem.at[1]),
        pltpu.make_async_copy(skip_hbm, skip_v, in_sem.at[2]),
    ]

    def xcopy(c):
        at = pl.ds(c * KCH, KCH)
        return pltpu.make_async_copy(x_hbm.at[:, at], xb.at[:, at], xi_sem.at[c])

    def wcopy(j, c):
        at = pl.ds(c * KCH, KCH)
        return pltpu.make_async_copy(w_hbm.at[j, at], wb.at[j, at], w_sem.at[j, c])

    def ocopy(k):
        p = rowpeer(k // 2, k % 2)
        return pltpu.make_async_copy(o_hbm.at[:, p], ob.at[k // 4, :, k % 4], o_sem)

    for c in range(NK):
        xcopy(c).start()
        wcopy(1, c).start()
        wcopy(2, c).start()
    for copy in copies:
        copy.start()

    barrier = pltpu.get_barrier_semaphore()

    def greet(c, t):
        pl.semaphore_signal(barrier, inc=1, device_id=(c, t), device_id_type=MESH)

    row_loop(lambda e, dc: greet(y * NX + rowpeer(e, dc), z))

    @pl.loop(1, 8)
    def _(o):
        greet((y + o) % NY * NX + xc, z)
        greet(ctx, (z + o) % NZ)

    greet(nxt, z)
    greet(prv, z)

    row = lax.broadcasted_iota(jnp.int32, (256, 256), 0)
    col = lax.broadcasted_iota(jnp.int32, (256, 256), 1)
    take = (row % 16 // 2 * 2 + row // 16 % 2) * 16 + row // 32 * 2 + row % 2
    perm1[...] = jnp.where(col == take, 1.0, 0.0).astype(bf16)
    row = lax.broadcasted_iota(jnp.int32, (128, 128), 0)
    col = lax.broadcasted_iota(jnp.int32, (128, 128), 1)
    perm2[...] = jnp.where(col == (row % 16 // 2) * 16 + row // 16 * 2 + row % 2, 1.0, 0.0).astype(bf16)
    pacc[...] = jnp.zeros_like(pacc)
    acc[...] = jnp.zeros_like(acc)
    for k in range(1, 8):
        lhs[: 16 * k, k * 256 : (k + 1) * 256] = jnp.zeros((16 * k, 256), bf16)
    toep[128 * 128 :, :] = jnp.zeros((128, 128), bf16)

    def send(src, dst, sems, c, t, k=1):
        return pltpu.make_async_remote_copy(
            src_ref=src, dst_ref=dst, send_sem=sems.at[0], recv_sem=sems.at[k],
            device_id=(c, t), device_id_type=MESH)

    def arrived(at, sems, k=1):
        send(at, at, sems, ctx, z, k).wait_recv()

    def left(at, sems):
        send(at, at, sems, ctx, z).wait_send()

    def row_exchange(src, dst, sems):
        def one(e, dc):
            p = rowpeer(e, dc)
            send(src.at[p], dst.at[xc], sems, y * NX + p, z).start()

        row_loop(one)

    def row_all(at):
        return at.at[pl.ds(0, NX - 1)]

    def col_exchange(src_of, dst, sems):
        @pl.loop(0, 7)
        def _(t):
            p = (y + chip(t)) % NY
            send(src_of(p), dst.at[y], sems, p * NX + xc, z).start()

    def col_all(at):
        return at.at[pl.ds(0, NY - 1)]


    def projected(j):
        rounded = pacc[j].astype(bf16)
        ext[j, 8:, :] = rounded.astype(f32)
        halo_s[j] = rounded[ROWS - 8 :, :]

    kv, q = pl.ds(1, 2), pl.ds(0, 1)

    def short_conv(j):
        before = halo_r[j].astype(f32)
        ext[j, :8, :] = jnp.where(ctx == 0, jnp.zeros_like(before), before)
        taps = [taps_v[i].astype(f32)[j : j + 1, :] for i in range(3)]
        return (
            taps[0] * ext[j, 8:, :]
            + taps[1] * ext[j, 7 : 7 + ROWS, :]
            + taps[2] * ext[j, 6 : 6 + ROWS, :]
        )

    copies[1].wait()
    for f in range(NX):
        fs[f] = filt_v[f : f + 1, :]

    @pl.loop(0, NK)
    def _(c):
        for copy in (xcopy(c), wcopy(1, c), wcopy(2, c)):
            copy.wait()
        at = pl.ds(pl.multiple_of(c * KCH, KCH), KCH)
        both = jnp.dot(
            xb[:, at], jnp.concatenate([wb[1, at, :], wb[2, at, :]], axis=1), preferred_element_type=f32
        )
        pacc[1] += both[:, :CHAN]
        pacc[2] += both[:, CHAN:]

    projected(1)
    projected(2)
    for c in range(NK):
        wcopy(0, c).start()
    pl.semaphore_wait(barrier, NX - 1 + NY - 1 + 2 + NZ - 1)
    send(halo_s.at[kv], halo_r.at[kv], halo_sem, nxt, z).start()

    row_exchange(fs, fr, f_sem)
    fr[xc] = fs[xc]
    copies[0].wait()
    copies[2].wait()
    arrived(halo_r.at[kv], halo_sem)
    keyed = short_conv(1)
    gated = keyed * short_conv(2)
    xs[...] = gated.T.astype(bf16).reshape(NX, 16, ROWS)
    row_exchange(xs, xr, x_sem)
    xr[xc] = xs[xc]

    arrived(row_all(fr), f_sem)
    hs[...] = fr[...].reshape(NX, ROWS)
    col_exchange(lambda p: hs, hr, h_sem)
    hr[y] = hs[...]

    direct_t[...] = (skip_v[...] * gated).T

    arrived(row_all(xr), x_sem)
    ys[...] = jnp.dot(
        perm1[...], xr[...].reshape(256, ROWS), preferred_element_type=f32
    ).astype(bf16).reshape(NY, 2, 16, ROWS)
    col_exchange(lambda p: ys.at[p], yr, y_sem)
    yr[y] = ys[y]

    @pl.loop(0, NX)
    def _(k):
        ocopy(k).start()


    lane = lax.broadcasted_iota(jnp.int32, (128, 128), 1)
    sub = lax.broadcasted_iota(jnp.int32, (128, 128), 0)
    keep = lane >= sub

    arrived(col_all(hr), h_sem)

    def toeplitz(p, before):
        for j in range(16):
            line = hr[p, j : j + 1, :]
            now = pltpu.roll(jnp.broadcast_to(line, (128, 128)), 0, 1, stride=1, stride_axis=0)
            at = pl.multiple_of((127 - j) * 128 - p * 2048, 128)
            toep[pl.ds(at, 128), :] = jnp.where(keep, now, before).astype(bf16)
            before = now
        return before

    lax.fori_loop(0, NY, toeplitz, jnp.zeros((128, 128), f32))

    arrived(col_all(yr), y_sem)
    for k in range(8):
        for p in range(8 - k):
            for par in range(2):
                at = k * 256 + par * 128
                lhs[16 * (p + k) : 16 * (p + k + 1), at : at + 128] = yr[p, par]

    @pl.loop(0, 4)
    def _(i):
        right = []
        for k in range(8):
            at = [pl.multiple_of(14464 - 2048 * k + 512 * i + r, 128) for r in (0, -128, 256, 128)]
            right.append(jnp.concatenate([toep[pl.ds(r, 256), :] for r in at], axis=1))
        both = jnp.dot(lhs[...], jnp.concatenate(right, axis=0), preferred_element_type=f32)
        acc[8:, :] = acc[6 : 6 + 128, :] + both[:, :256]
        acc[8:, :] = acc[6 : 6 + 128, :] + both[:, 256:]

    ys2[...] = acc[8:, :].astype(bf16).reshape(NY, 16, 256)
    col_exchange(lambda p: ys2.at[p], yr2, y2_sem)
    yr2[y] = ys2[y]
    @pl.loop(0, NK)
    def _(c):
        wcopy(0, c).wait()
        at = pl.ds(pl.multiple_of(c * KCH, KCH), KCH)
        pacc[0] += jnp.dot(xb[:, at], wb[0, at, :], preferred_element_type=f32)

    projected(0)
    send(halo_s.at[q], halo_r.at[q], halo_sem, nxt, z, 2).start()
    pltpu.make_async_copy(ob, ob, o_sem).wait()
    left(row_all(fs), f_sem)
    left(row_all(xs), x_sem)
    left(col_all(hr), h_sem)
    left(col_all(ys), y_sem)
    arrived(col_all(yr2), y2_sem)
    back = jnp.dot(
        perm2[...], yr2[...].reshape(128, 256), preferred_element_type=f32
    ).astype(bf16)
    for b in range(8):
        for par in range(2):
            xs2[2 * b + par] = back[16 * b : 16 * b + 16, 128 * par : 128 * par + 128]
    def give(e, dc):
        p = rowpeer(e, dc)
        there = (8 - e) % 8
        send(xs2.at[p], xr2.at[2 * there + dc], x2_sem, y * NX + p, z, 1 + there // 2).start()

    row_loop(give)
    xr2[0] = xs2[xc]
    arrived(halo_r.at[q], halo_sem, 2)
    query_t[...] = short_conv(0).T
    left(halo_s, halo_sem)

    def zsend(g, o_block, o_to, k=None):
        at = hid.at[g, (z + o_block) % NZ]
        send(at, at, z_sem, ctx, (z + o_to) % NZ, 1 + g if k is None else k).start()

    relayed = (0, 3, 1)

    def own(g):
        arrived(xr2.at[pl.ds(1, 3) if g == 0 else pl.ds(4 * g, 4)], x2_sem, 1 + g)
        for k in range(4):
            at = pl.ds(pl.multiple_of(rowpeer(2 * g + k // 2, k % 2) * 16, 16), 16)
            hid[g, z, k] = (query_t[at, :] * (xr2[4 * g + k].astype(f32) + direct_t[at, :])).astype(bf16)
        if g not in relayed:
            zsend(g, 0, 4)
            zsend(g, 0, 5)
        else:
            zsend(g, 0, 5, 5 + g)
        for o in (3, 6, 2, 7, 1):
            zsend(g, 0, o)

    def relay(g):
        arrived(hid.at[g, (z + 3) % NZ], z_sem, 5 + g)
        zsend(g, 3, 7)

    def out_part(g):
        arrived(hid.at[g, pl.ds(0, 6 if g in relayed else 7)], z_sem, 1 + g)
        return lax.dot_general(
            hid[g].reshape(NZ * 64, ROWS), ob[g].reshape(NZ * 64, FEATS),
            (((0,), (0,)), ((), ())), preferred_element_type=f32)

    for g in (0, 3, 1, 2):
        own(g)
    for g in relayed:
        relay(g)
    oacc[...] = out_part(0)
    oacc[...] += out_part(3)
    oacc[...] += out_part(1)
    left(col_all(ys2), y2_sem)
    left(row_all(xs2), x2_sem)
    out_ref[...] = (oacc[...] + out_part(2)).astype(bf16)
    for g in range(4):
        left(hid.at[g, pl.ds(0, 7)], z_sem)


def per_device(hidden_in, in_proj, short_taps, long_filters, skip_gain, out_proj):
    f32, bf16 = jnp.float32, jnp.bfloat16
    VMEM, DMA = pltpu.VMEM, pltpu.SemaphoreType.DMA
    scratch = [
        VMEM((ROWS, MODEL), bf16),
        VMEM((3, MODEL, CHAN), bf16),
        VMEM((4, NZ, 4, 16, FEATS), bf16),
        VMEM((3, 3, CHAN), bf16),
        VMEM((NX, ROWS), f32),
        VMEM((1, CHAN), f32),
        VMEM((3, ROWS, CHAN), f32),
        VMEM((3, 8, CHAN), bf16),
        VMEM((3, 8, CHAN), bf16),
        VMEM((3, ROWS + 8, CHAN), f32),
        VMEM((CHAN, ROWS), f32),
        VMEM((CHAN, ROWS), f32),
        VMEM((NX, 1, ROWS), f32),
        VMEM((NX, 1, ROWS), f32),
        VMEM((NX, ROWS), f32),
        VMEM((NY, NX, ROWS), f32),
        VMEM((TOEP, 128), bf16),
        VMEM((256, 256), bf16),
        VMEM((128, 128), bf16),
        VMEM((128, 2048), bf16),
        VMEM((NX, 16, ROWS), bf16),
        VMEM((NX, 16, ROWS), bf16),
        VMEM((NY, 2, 16, ROWS), bf16),
        VMEM((NY, 2, 16, ROWS), bf16),
        VMEM((136, 256), f32),
        VMEM((NY, 16, 256), bf16),
        VMEM((NY, 16, 256), bf16),
        VMEM((NX, 16, ROWS), bf16),
        VMEM((NX, 16, ROWS), bf16),
        VMEM((4, NZ, 4, 16, ROWS), bf16),
        VMEM((ROWS, FEATS), f32),
        DMA((3,)),
        DMA((NK,)),
        DMA((3, NK)),
        DMA,
        DMA((3,)),
        DMA((2,)),
        DMA((2,)),
        DMA((2,)),
        DMA((2,)),
        DMA((2,)),
        DMA((5,)),
        DMA((9,)),
    ]
    return pl.pallas_call(
        kernel,
        out_shape=jax.ShapeDtypeStruct((ROWS, FEATS), bf16),
        in_specs=[pl.BlockSpec(memory_space=pl.ANY)] * 6,
        out_specs=pl.BlockSpec(memory_space=pltpu.VMEM),
        scratch_shapes=scratch,
        compiler_params=pltpu.CompilerParams(
            collective_id=0, has_side_effects=True, vmem_limit_bytes=67043328
        ),
    )(
        hidden_in,
        jnp.transpose(in_proj, (1, 0, 2)),
        short_taps,
        long_filters.T,
        skip_gain.reshape(1, CHAN),
        out_proj.reshape(NZ, NX, 16, FEATS),
    )


def solution(mesh):
    in_specs = (
        P("ctx", None),
        P(None, None, "tp"),
        P(None, None, "tp"),
        P("ctx", "tp"),
        P("tp"),
        P(None, "tp"),
    )
    return jax.shard_map(
        per_device, mesh=mesh, in_specs=in_specs, out_specs=P("ctx", "tp"), check_vma=False
    )
```
